32 devices in a mesh: groups: 2 (over x), dp: 16 (over z, y, core).
Axes of the slice: x: 2, y: 2, z: 4, core: 2. Of those that a mesh axis runs over, the one named last changes fastest.
Arguments:
- hidden_input_rows: bfloat16 [8192, 8192], P(('groups', 'dp')), parts along dimension 0, may hold values from -6 to 6
- rank_cotangent: bfloat16 [8192, 128], P(('groups', 'dp')), parts along dimension 0, may hold values from -0.25 to 0.25
- token_identifiers: int32 [8192], P(('groups', 'dp')), parts along dimension 0, may hold values from 0 to 31999, as said below
- adam_first_moment: float32 [8192, 128], P('dp'), may hold values from -0.6 to 0.6
- adam_second_moment: float32 [8192, 128], P('dp'), may hold values from 0.0001 to 0.01
- block_seeds: int32 [8], replicated, may hold values from 0 to 1073741823
Outputs:
- feature_rows: float32 [32, 2048], P(('groups', 'dp')), parts along dimension 0
The draws below stay inside these ranges and needn't reach their ends.
There are 2 independent parts, one for each index of `groups`. The reference program is written for one: setup_inputs(seed, part) draws one part's arguments, and reference() takes and returns one part's arrays. A program takes and returns all parts, laid end to end along the dimension named above; an argument that names none is the same for every part. Nothing has to cross between parts.
Inputs may be any that keep to these rules, and one draw needn't show every extreme that they name: `token_identifiers`: 0 marks padding. In each sequence of 512 positions the real tokens (ids 1 and up) come first and number at least 128; the rest is padding. Some sequence has no padding.
All inputs are finite; a program needn't handle non-finite values.
Results may differ from the reference program's by a relative error of at most 0.0029.
Values sent between devices are 32-bit elements; how exact they have to be, the bound alone decides.
No kernel may reach another device: no remote copies, remote signals or barrier semaphores. Data moves between devices by JAX's collectives and lax.ppermute only.
A program may use at most 64 MiB of HBM per device.

```python
import math
import jax
import jax.numpy as jnp
from jax import lax

D = 8192
VOCAB = 32000
ADAPTER_RANK = 128
K = 4096
FEAT_BLOCK = 512
SEQ_LEN = 512
SEQS = 8
TOKEN_TOTAL = 4096


def draw_token_identifiers(key, part):
    key_lengths = jax.random.fold_in(key, 11)
    key_full = jax.random.fold_in(key, 12)
    key_values = jax.random.fold_in(key, 13)
    lengths = jax.random.randint(key_lengths, (SEQS,), SEQ_LEN // 4, SEQ_LEN + 1, dtype=jnp.int32)
    full_row = jax.random.randint(key_full, (), 0, SEQS, dtype=jnp.int32)
    lengths = jnp.where(jnp.arange(SEQS, dtype=jnp.int32) == full_row, SEQ_LEN, lengths)
    token_values = jax.random.randint(key_values, (SEQS, SEQ_LEN), 1, VOCAB, dtype=jnp.int32)
    positions = jnp.arange(SEQ_LEN, dtype=jnp.int32)[None, :]
    return jnp.where(positions < lengths[:, None], token_values, 0).reshape(TOKEN_TOTAL)


def plant(values, key, smallest, top_value):
    shape = values.shape
    index_at = [jax.random.randint(jax.random.fold_in(key, axis), (), 0, shape[axis]) for axis in range(len(shape))]
    values = values.at[tuple(index_at)].set(smallest)
    longest = shape.index(max(shape))
    index_at[longest] = (index_at[longest] + 1) % shape[longest]
    return values.at[tuple(index_at)].set(top_value)


def block_scale(key, extent, pieces, smallest, high):
    def one(axis_at, parts):
        steps = jax.random.uniform(jax.random.fold_in(jax.random.fold_in(key, 6), axis_at), (parts,), jnp.float32, smallest / len(pieces), high / len(pieces))
        return jnp.repeat(jnp.exp(steps), extent[axis_at] // parts).reshape((-1,) + (1,) * (len(extent) - axis_at - 1))

    gain = one(*pieces[0])
    for cut in pieces[1:]:
        gain = gain * one(*cut)
    return gain


def centred(stream_key, dims, scale, limit, pieces=(), held_as=jnp.bfloat16):
    gain = block_scale(stream_key, dims, pieces, -0.22, 0.18) if pieces else 1.0
    entries = jax.random.normal(stream_key, dims, jnp.float32) * scale * gain
    return jnp.minimum(jnp.maximum(entries, -limit), limit).astype(held_as)


def setup_inputs(seed: int = 0, part: int = 0) -> dict:
    streams_of = jax.random.split(jax.random.key(seed), 7)
    part_splits = jax.random.split(jax.random.fold_in(streams_of[6], part), 7)
    hidden_input_rows = centred(part_splits[0], (TOKEN_TOTAL, D), 1.0, 6.0, ((0, 16),))
    rank_cotangent = centred(part_splits[1], (TOKEN_TOTAL, ADAPTER_RANK), 0.03125, 0.25, ((0, 16),))
    token_identifiers = draw_token_identifiers(jax.random.fold_in(jax.random.fold_in(streams_of[6], part), 71), part)
    adam_first_moment = centred(streams_of[3], (D, ADAPTER_RANK), 0.1, 0.6, ((0, 16),), jnp.float32)
    adam_second_moment = jnp.clip(jnp.exp(math.log(0.01) - 4.6051702 * jax.random.uniform(streams_of[4], (D, ADAPTER_RANK), jnp.float32) ** block_scale(streams_of[4], (D, ADAPTER_RANK), ((0, 16),), -0.2, 0.2)), 0.0001, 0.01)
    block_seeds = plant(jax.random.randint(streams_of[5], (K // FEAT_BLOCK,), 0, 1073741824), jax.random.fold_in(streams_of[5], 1), 0, 1073741823).astype(jnp.int32)
    return {"hidden_input_rows": hidden_input_rows, "rank_cotangent": rank_cotangent, "token_identifiers": token_identifiers, "adam_first_moment": adam_first_moment, "adam_second_moment": adam_second_moment, "block_seeds": block_seeds}


beta_one = 0.9
beta_two = 0.999
epsilon = 1e-08
mix_feature = 1640531527
mix_param = 2028178513
mix_round = 73244475

def scramble(hashed):
    hashed = hashed ^ lax.shift_right_logical(hashed, jnp.full_like(hashed, 16))
    hashed = hashed * mix_round
    hashed = hashed ^ lax.shift_right_logical(hashed, jnp.full_like(hashed, 16))
    hashed = hashed * mix_round
    hashed = hashed ^ lax.shift_right_logical(hashed, jnp.full_like(hashed, 16))
    return hashed

def sign_block(seed_values, feature_index, param_index):
    hashed = seed_values[:, None] + feature_index[:, None] * mix_feature + param_index[None, :] * mix_param
    hashed = scramble(hashed)
    return 1 - 2 * lax.shift_right_logical(hashed, jnp.full_like(hashed, 31))

def reference(hidden_input_rows, rank_cotangent, token_identifiers, adam_first_moment, adam_second_moment, block_seeds):
    padding_mask = (token_identifiers != 0).astype(jnp.bfloat16)
    masked_values = rank_cotangent * padding_mask[:, None]
    inputs_seq = hidden_input_rows.reshape(SEQS, SEQ_LEN, D)
    masked_seq = masked_values.reshape(SEQS, SEQ_LEN, ADAPTER_RANK)

    def one_grad(pair_args):
        return jnp.dot(pair_args[0].T, pair_args[1], preferred_element_type=jnp.float32)
    gradient = lax.map(one_grad, (inputs_seq, masked_seq))
    moment_one = beta_one * adam_first_moment[None] + (1 - beta_one) * gradient
    moment_two = beta_two * adam_second_moment[None] + (1 - beta_two) * gradient * gradient
    direction = (moment_one / (jnp.sqrt(moment_two) + epsilon)).astype(jnp.bfloat16)
    direction = lax.optimization_barrier(direction).astype(jnp.float32).reshape(SEQS, D * ADAPTER_RANK)
    seed_values = jnp.repeat(block_seeds, FEAT_BLOCK)
    feature_index = jnp.arange(K, dtype=jnp.int32)
    param_block = math.gcd(D * ADAPTER_RANK, 8192)

    def accumulate(block_number, running):
        start_param = (block_number * param_block).astype(jnp.int32)
        param_index = start_param + jnp.arange(param_block, dtype=jnp.int32)
        sign_tile = sign_block(seed_values, feature_index, param_index).astype(jnp.float32)
        direction_piece = lax.dynamic_slice_in_dim(direction, start_param, param_block, 1)
        return running + lax.dot_general(direction_piece, sign_tile, (((1,), (1,)), ((), ())), precision=lax.Precision.HIGHEST, preferred_element_type=jnp.float32)
    features = lax.fori_loop(jnp.int32(0), jnp.int32(D * ADAPTER_RANK // param_block), accumulate, jnp.zeros((SEQS, K), jnp.float32))
    features = features * (1.0 / math.sqrt(D * ADAPTER_RANK))
    return features.reshape(SEQS * 2, K // 2)
```

```python
import functools
import math

import jax
import jax.numpy as jnp
from jax import lax
from jax.experimental import pallas as pl
from jax.experimental.pallas import tpu as pltpu
from jax.sharding import PartitionSpec as P

FEAT_BLOCK = 512
beta_one = 0.9
beta_two = 0.999
epsilon = 1e-08
mix_feature = 1640531527
mix_param = 2028178513
mix_round = 73244475
DIGITS = 4
RADIX = 16.0
FP8 = jnp.float8_e4m3fn
STEP_ROWS = 2048
KEPT_ROWS = 512
TILE_ROWS = 512
TILE_FEATS = 2048


def wrap(value):
    value &= 0xFFFFFFFF
    return jnp.int32(value - (1 << 32) if value >= (1 << 31) else value)


def scramble(hashed):
    hashed = hashed ^ lax.shift_right_logical(hashed, jnp.full_like(hashed, 16))
    hashed = hashed * mix_round
    hashed = hashed ^ lax.shift_right_logical(hashed, jnp.full_like(hashed, 16))
    return hashed * mix_round


def first_param(rows, groups, rank):
    mine = lax.axis_index("dp") * groups + lax.axis_index("groups")
    return mine * (rows * rank)


def hash_base(seed_ref, feature_tile, start):
    pieces = []
    for piece in range(TILE_FEATS // FEAT_BLOCK):
        block = feature_tile * (TILE_FEATS // FEAT_BLOCK) + piece
        down = lax.broadcasted_iota(jnp.int32, (8, FEAT_BLOCK), 0)
        across = lax.broadcasted_iota(jnp.int32, (8, FEAT_BLOCK), 1)
        scalar = seed_ref[block] + block * wrap(FEAT_BLOCK * mix_feature) + start * wrap(mix_param)
        pieces.append(down * wrap(mix_param) + across * wrap(mix_feature) + scalar)
    return jnp.concatenate(pieces, axis=1)


def write_signs(base, rows, out_ref):
    for top in range(0, rows, 32):
        hashes = [scramble(base + wrap(mix_param * (top + 8 * part))) for part in range(4)]
        hashed = jnp.concatenate(hashes, axis=0)
        out_ref[pl.ds(top, 32), :] = jnp.where(hashed < 0, FP8(-1), FP8(1))


def gradient_kernel(side_ref, inputs_ref, masked_ref, out_ref):
    out_ref[0] = lax.dot_general(
        inputs_ref[...],
        masked_ref[...],
        (((0,), (0,)), ((), ())),
        preferred_element_type=jnp.float32,
    )


def gradient_sum_kernel(side_ref, inputs_ref, masked_ref, other_ref, out_ref):
    out_ref[0] = other_ref[0] + lax.dot_general(
        inputs_ref[...],
        masked_ref[...],
        (((0,), (0,)), ((), ())),
        preferred_element_type=jnp.float32,
    )


def half_gradient(inputs, masked, side, groups, rows, other=None):
    tokens, width = inputs.shape
    rank = masked.shape[1]
    pairs = width // (2 * groups * rows)
    shape = (groups * pairs, rows, rank)
    if rows % 128:
        whole = lax.dot_general(
            inputs, masked, (((0,), (0,)), ((), ())), preferred_element_type=jnp.float32
        )
        whole = whole.reshape(pairs, 2, groups, rows, rank)
        mine = lax.dynamic_index_in_dim(whole, side, 1, keepdims=False).swapaxes(0, 1).reshape(shape)
        return mine if other is None else mine + other
    block_map = lambda pair, group, side_ref: (group * pairs + pair, 0, 0)
    in_specs = [
        pl.BlockSpec(
            (tokens, rows), lambda pair, group, side_ref: (0, (2 * pair + side_ref[0]) * groups + group)
        ),
        pl.BlockSpec((tokens, rank), lambda pair, group, side_ref: (0, 0)),
    ]
    operands = [inputs, masked]
    if other is not None:
        in_specs.append(pl.BlockSpec((1, rows, rank), block_map))
        operands.append(other)
    return pl.pallas_call(
        gradient_kernel if other is None else gradient_sum_kernel,
        grid_spec=pltpu.PrefetchScalarGridSpec(
            num_scalar_prefetch=1,
            grid=(pairs, groups),
            in_specs=in_specs,
            out_specs=pl.BlockSpec((1, rows, rank), block_map),
        ),
        out_shape=jax.ShapeDtypeStruct(shape, jnp.float32),
        cost_estimate=pl.CostEstimate(
            flops=tokens * width * rank, bytes_accessed=tokens * width + 4 * width * rank, transcendentals=0
        ),
        name="half_gradient",
    )(side[None], *operands)


def signs_kernel(rows, groups, rank, seed_ref, out_ref):
    start = first_param(rows, groups, rank) + pl.program_id(0) * STEP_ROWS
    write_signs(hash_base(seed_ref, pl.program_id(1), start), KEPT_ROWS, out_ref)


def kept_signs(seeds, rows, groups, rank):
    steps = rows * rank // STEP_ROWS
    features = seeds.shape[0] * FEAT_BLOCK
    total = steps * KEPT_ROWS * features
    return pl.pallas_call(
        functools.partial(signs_kernel, rows, groups, rank),
        grid=(steps, features // TILE_FEATS),
        in_specs=[pl.BlockSpec(memory_space=pltpu.SMEM)],
        out_specs=pl.BlockSpec((KEPT_ROWS, TILE_FEATS), lambda step, tile: (step, tile)),
        out_shape=jax.ShapeDtypeStruct((steps * KEPT_ROWS, features), FP8),
        cost_estimate=pl.CostEstimate(flops=total * 10, bytes_accessed=total, transcendentals=0),
        name="kept_signs",
    )(seeds)


def direction_kernel(rows, gradient_ref, first_ref, second_ref, out_ref, scale_ref, held):
    sequences, rank = gradient_ref.shape[0], gradient_ref.shape[2]
    start = lax.axis_index("groups") * rows

    def moments(block, largest):
        at = pl.ds(pl.multiple_of(block * 8, 8), 8)
        here = pl.ds(pl.multiple_of(start + block * 8, 8), 8)
        gradient = gradient_ref[:, at, :]
        moment_one = beta_one * first_ref[here, :][None] + (1 - beta_one) * gradient
        moment_two = beta_two * second_ref[here, :][None] + (1 - beta_two) * gradient * gradient
        direction = moment_one / (jnp.sqrt(moment_two) + epsilon)
        direction = direction.astype(jnp.bfloat16).astype(jnp.float32)
        direction = jnp.swapaxes(direction, 0, 1)
        for row in range(8):
            held[block * 8 + row] = direction[row]
        return jnp.maximum(largest, jnp.max(jnp.abs(direction), axis=0))

    largest = lax.fori_loop(0, rows // 8, moments, jnp.zeros((sequences, rank), jnp.float32))
    largest = jnp.broadcast_to(jnp.max(largest, axis=1, keepdims=True), (sequences, rank))
    scale = jnp.ones_like(largest)
    for power in (64, 32, 16, 8, 4, 2, 1):
        room = largest * (2.0**power) < RADIX
        largest = jnp.where(room, largest * (2.0**power), largest)
        scale = jnp.where(room, scale * (2.0**power), scale)
    for power in (2, 1):
        over = largest >= RADIX
        largest = jnp.where(over, largest * (0.5**power), largest)
        scale = jnp.where(over, scale * (0.5**power), scale)
    scale_ref[...] = scale

    def split(row, _):
        rest = held[row] * scale
        digits = []
        for _ in range(DIGITS):
            digit = jnp.round(rest)
            digits.append(digit)
            rest = (rest - digit) * RADIX
        out_ref[:, pl.ds(pl.multiple_of(row * rank, rank), rank)] = jnp.concatenate(digits, axis=0).astype(FP8)
        return 0

    lax.fori_loop(0, rows, split, 0, unroll=8)


def scaled_direction(gradient, first, second, rows):
    sequences, _, rank = gradient.shape
    return pl.pallas_call(
        functools.partial(direction_kernel, rows),
        out_shape=(
            jax.ShapeDtypeStruct((DIGITS * sequences, rows * rank), FP8),
            jax.ShapeDtypeStruct((sequences, rank), jnp.float32),
        ),
        scratch_shapes=[pltpu.VMEM((rows, sequences, rank), jnp.float32)],
        compiler_params=pltpu.CompilerParams(vmem_limit_bytes=48 << 20),
        cost_estimate=pl.CostEstimate(
            flops=20 * gradient.size, bytes_accessed=5 * gradient.size, transcendentals=2 * gradient.size
        ),
        name="direction",
    )(gradient, first, second)


def project_kernel(rows, groups, rank, final_scale, seed_ref, direction_ref, scale_ref, kept_ref, out_ref, total, *tiles):
    tile, step = pl.program_id(0), pl.program_id(1)
    sequences = scale_ref.shape[0]
    start = first_param(rows, groups, rank) + step * STEP_ROWS
    count = len(tiles)

    def multiply(at, signs):
        at = pl.multiple_of(at, TILE_ROWS)
        total[...] += jnp.dot(
            direction_ref[:, pl.ds(at, signs.shape[0])], signs[...], preferred_element_type=jnp.float32
        )

    @pl.when(step == 0)
    def _():
        total[...] = jnp.zeros_like(total)
        tiles[-1][...] = jnp.zeros_like(tiles[-1])

    here = step * STEP_ROWS
    for index in range(count):
        offset = KEPT_ROWS + index * TILE_ROWS
        write_signs(hash_base(seed_ref, tile, start + offset), TILE_ROWS, tiles[index])
        if index == 0:
            multiply(jnp.maximum(here - TILE_ROWS, 0), tiles[-1])
            multiply(here, kept_ref)
        else:
            multiply(here + offset - TILE_ROWS, tiles[index - 1])

    @pl.when(step == pl.num_programs(1) - 1)
    def _():
        multiply(here + STEP_ROWS - TILE_ROWS, tiles[-1])
        inverse = (1.0 / scale_ref[...])[:, :1]
        value = total[(DIGITS - 1) * sequences :, :]
        for digit in reversed(range(DIGITS - 1)):
            value = total[digit * sequences : (digit + 1) * sequences, :] + value * (1.0 / RADIX)
        out_ref[...] = value * inverse * final_scale


def project(seeds, direction, scale, kept, rows, groups, rank, final_scale):
    features = seeds.shape[0] * FEAT_BLOCK
    sequences = scale.shape[0]
    params = rows * rank
    steps = params // STEP_ROWS
    count = (STEP_ROWS - KEPT_ROWS) // TILE_ROWS
    return pl.pallas_call(
        functools.partial(project_kernel, rows, groups, rank, final_scale),
        grid=(features // TILE_FEATS, steps),
        in_specs=[
            pl.BlockSpec(memory_space=pltpu.SMEM),
            pl.BlockSpec((DIGITS * sequences, params), lambda tile, step: (0, 0)),
            pl.BlockSpec((sequences, rank), lambda tile, step: (0, 0)),
            pl.BlockSpec((KEPT_ROWS, TILE_FEATS), lambda tile, step: (step, tile)),
        ],
        out_specs=pl.BlockSpec((sequences, TILE_FEATS), lambda tile, step: (0, tile)),
        out_shape=jax.ShapeDtypeStruct((sequences, features), jnp.float32),
        scratch_shapes=[pltpu.VMEM((DIGITS * sequences, TILE_FEATS), jnp.float32)]
        + [pltpu.VMEM((TILE_ROWS, TILE_FEATS), FP8)] * count,
        cost_estimate=pl.CostEstimate(
            flops=10 * params * features, bytes_accessed=params * features // 4, transcendentals=0
        ),
        name="project",
    )(seeds, direction, scale, kept)


def local(
    hidden_input_rows,
    rank_cotangent,
    token_identifiers,
    adam_first_moment,
    adam_second_moment,
    block_seeds,
):
    groups, device_list = lax.axis_size("groups"), lax.axis_size("dp")
    hidden_width = hidden_input_rows.shape[1]
    rank = rank_cotangent.shape[1]
    rows = adam_first_moment.shape[0] // groups
    features = block_seeds.shape[0] * FEAT_BLOCK
    core = lax.axis_index("dp") & 1
    padding_mask = (token_identifiers != 0).astype(jnp.bfloat16)
    masked = rank_cotangent * padding_mask[:, None]

    given = half_gradient(hidden_input_rows, masked, 1 - core, groups, rows)
    pairs = [(source, source ^ 1) for source in range(device_list)]
    other = lax.ppermute(given, "dp", pairs)
    summed = half_gradient(hidden_input_rows, masked, core, groups, rows, other)
    kept = kept_signs(block_seeds, rows, groups, rank)

    half = device_list // 2
    everyone = [
        [group * device_list + 2 * pair + side for group in range(groups) for pair in range(half)]
        for side in range(2)
    ]
    gradient = lax.all_to_all(
        summed, ("groups", "dp"), split_axis=0, concat_axis=0, axis_index_groups=everyone, tiled=True
    )
    direction, scale = scaled_direction(gradient, adam_first_moment, adam_second_moment, rows)
    final_scale = 1.0 / math.sqrt(hidden_width * rank)
    partial = project(block_seeds, direction, scale, kept, rows, groups, rank, final_scale)
    partial = partial.reshape(groups * device_list, features // 2)
    partial = lax.all_to_all(partial, ("groups", "dp"), split_axis=0, concat_axis=0, tiled=True)
    return jnp.sum(partial, axis=0, keepdims=True)


def solution(mesh):
    in_specs = (
        P(("groups", "dp"), None),
        P(("groups", "dp"), None),
        P(("groups", "dp")),
        P("dp", None),
        P("dp", None),
        P(),
    )
    out_specs = P(("groups", "dp"), None)
    return jax.shard_map(local, mesh=mesh, in_specs=in_specs, out_specs=out_specs, check_vma=False)
```

```python
import functools
import math

import jax
import jax.numpy as jnp
from jax import lax
from jax.experimental import pallas as pl
from jax.experimental.pallas import tpu as pltpu
from jax.sharding import PartitionSpec as P

FEAT_BLOCK = 512
beta_one = 0.9
beta_two = 0.999
epsilon = 1e-08
mix_feature = 1640531527
mix_param = 2028178513
mix_round = 73244475
DIGITS = 4
RADIX = 16.0
FP8 = jnp.float8_e4m3fn
STEP_ROWS = 4096
KEPT_ROWS = 1280
TILES = (768, 768, 768, 512)
EARLY_BLOCKS = 2
TILE_FEATS = 2048


def wrap(value):
    value &= 0xFFFFFFFF
    return jnp.int32(value - (1 << 32) if value >= (1 << 31) else value)


def scramble(hashed):
    hashed = hashed ^ lax.shift_right_logical(hashed, jnp.full_like(hashed, 16))
    hashed = hashed * mix_round
    hashed = hashed ^ lax.shift_right_logical(hashed, jnp.full_like(hashed, 16))
    return hashed * mix_round


def strides(rows, rank):
    return (1, rank) if rows % 128 == 0 else (rank, 1)


def minor_size(rows, rank):
    return rows if rows % 128 == 0 else rank


def step_start(rows, rank, groups, step):
    mine = lax.axis_index("dp") * groups + lax.axis_index("groups")
    return mine * (rows * rank) + step * (STEP_ROWS // minor_size(rows, rank) * strides(rows, rank)[0])


def hash_base(seed_ref, feature_tile, start, minor_stride):
    pieces = []
    for piece in range(TILE_FEATS // FEAT_BLOCK):
        block = feature_tile * (TILE_FEATS // FEAT_BLOCK) + piece
        down = lax.broadcasted_iota(jnp.int32, (8, FEAT_BLOCK), 0)
        across = lax.broadcasted_iota(jnp.int32, (8, FEAT_BLOCK), 1)
        scalar = seed_ref[block] + block * wrap(FEAT_BLOCK * mix_feature) + start * wrap(mix_param)
        pieces.append(down * wrap(mix_param * minor_stride) + across * wrap(mix_feature) + scalar)
    return jnp.concatenate(pieces, axis=1)


def write_signs(base, rows, rank, offset, count, out_ref):
    minor, (major_stride, minor_stride) = minor_size(rows, rank), strides(rows, rank)
    for top in range(0, count, 32):
        hashes = []
        for part in range(offset + top, offset + top + 32, 8):
            apart = part // minor * major_stride + part % minor * minor_stride
            hashes.append(scramble(base + wrap(mix_param * apart)))
        hashed = jnp.concatenate(hashes, axis=0)
        out_ref[pl.ds(top, 32), :] = jnp.where(hashed < 0, FP8(-1), FP8(1))


def gradient_kernel(side_ref, inputs_ref, cotangent_ref, tokens_ref, *refs):
    *other_refs, out_ref, masked = refs
    other_refs = other_refs[:1]

    @pl.when(pl.program_id(0) == 0)
    def _():
        turned = cotangent_ref[...].astype(jnp.float32).T
        masked[...] = jnp.where(tokens_ref[...] != 0, turned, 0.0).astype(jnp.bfloat16)

    part = jnp.dot(masked[...], inputs_ref[...], preferred_element_type=jnp.float32)
    groups, rows = out_ref.shape[0], out_ref.shape[3]
    for group in range(groups):
        piece = part[:, group * rows : (group + 1) * rows]
        for other_ref in other_refs:
            piece = piece + other_ref[group, 0]
        out_ref[group, 0] = piece


def half_gradient(inputs, cotangent, tokens, side, groups, rows, other=None, after=None):
    count, width = inputs.shape
    rank = cotangent.shape[1]
    pairs = width // (2 * groups * rows)
    if rows % 128:
        masked = jnp.where((tokens != 0)[:, None], cotangent, jnp.bfloat16(0))
        whole = lax.dot_general(
            inputs, masked, (((0,), (0,)), ((), ())), preferred_element_type=jnp.float32
        )
        whole = whole.reshape(pairs, 2, groups, rows, rank)
        mine = lax.dynamic_index_in_dim(whole, side, 1, keepdims=False).swapaxes(0, 1)
        if other is None:
            return mine
        other, _ = lax.optimization_barrier((other, after))
        return mine + other
    block = pl.BlockSpec((groups, 1, rank, rows), lambda pair, side_ref: (0, pair, 0, 0))
    in_specs = [
        pl.BlockSpec((count, groups * rows), lambda pair, side_ref: (0, 2 * pair + side_ref[0])),
        pl.BlockSpec((count, rank), lambda pair, side_ref: (0, 0)),
        pl.BlockSpec((1, count), lambda pair, side_ref: (0, 0)),
    ]
    operands = [inputs, cotangent, tokens[None, :]]
    if other is not None:
        in_specs += [block, pl.BlockSpec(memory_space=pl.ANY)]
        operands += [other, after]
    return pl.pallas_call(
        gradient_kernel,
        grid_spec=pltpu.PrefetchScalarGridSpec(
            num_scalar_prefetch=1,
            grid=(pairs,),
            in_specs=in_specs,
            out_specs=block,
            scratch_shapes=[pltpu.VMEM((rank, count), jnp.bfloat16)],
        ),
        out_shape=jax.ShapeDtypeStruct((groups, pairs, rank, rows), jnp.float32),
        compiler_params=pltpu.CompilerParams(vmem_limit_bytes=8 << 20),
        cost_estimate=pl.CostEstimate(
            flops=count * width * rank, bytes_accessed=count * width + 4 * width * rank, transcendentals=0
        ),
        name="half_gradient",
    )(side[None], *operands)


def signs_kernel(rows, groups, rank, first, seed_ref, *refs):
    block = first + pl.program_id(0)
    tiles = seed_ref.shape[0] * FEAT_BLOCK // TILE_FEATS
    start = step_start(rows, rank, groups, block // tiles)
    base = hash_base(seed_ref, block % tiles, start, strides(rows, rank)[1])
    write_signs(base, rows, rank, 0, KEPT_ROWS, refs[-1])


def kept_signs(seeds, rows, groups, rank, first, count, after, alias):
    features = seeds.shape[0] * FEAT_BLOCK
    steps, tiles = rows * rank // STEP_ROWS, features // TILE_FEATS
    size = count * KEPT_ROWS * TILE_FEATS
    return pl.pallas_call(
        functools.partial(signs_kernel, rows, groups, rank, first),
        grid=(count,),
        in_specs=[pl.BlockSpec(memory_space=pltpu.SMEM)]
        + [pl.BlockSpec(memory_space=pl.ANY)],
        out_specs=pl.BlockSpec(
            (KEPT_ROWS, TILE_FEATS), lambda index: ((index + first) // tiles, (index + first) % tiles)
        ),
        out_shape=jax.ShapeDtypeStruct((steps * KEPT_ROWS, features), FP8),
        input_output_aliases={1: 0} if alias else {},
        compiler_params=pltpu.CompilerParams(vmem_limit_bytes=16 << 20),
        cost_estimate=pl.CostEstimate(flops=size * 10, bytes_accessed=size, transcendentals=0),
        name="kept_signs",
    )(seeds, after)


def direction_kernel(rows, gradient_ref, first_ref, second_ref, out_ref, scale_ref, held, first, second):
    sequences, major, minor = gradient_ref.shape
    mine = pl.ds(pl.multiple_of(lax.axis_index("groups") * rows, 8), rows)
    turn = major != rows
    first[...] = first_ref[mine, :].T if turn else first_ref[mine, :]
    second[...] = second_ref[mine, :].T if turn else second_ref[mine, :]

    def moments(block, largest):
        at = pl.ds(pl.multiple_of(block * 8, 8), 8)
        gradient = gradient_ref[:, at, :]
        moment_one = beta_one * first[at, :][None] + (1 - beta_one) * gradient
        moment_two = beta_two * second[at, :][None] + (1 - beta_two) * gradient * gradient
        direction = moment_one / (jnp.sqrt(moment_two) + epsilon)
        direction = direction.astype(jnp.bfloat16).astype(jnp.float32)
        direction = jnp.swapaxes(direction, 0, 1)
        for row in range(8):
            held[block * 8 + row] = direction[row]
        return jnp.maximum(largest, jnp.max(jnp.abs(direction), axis=0))

    largest = lax.fori_loop(0, major // 8, moments, jnp.zeros((sequences, minor), jnp.float32))
    largest = jnp.broadcast_to(jnp.max(largest, axis=1, keepdims=True), (sequences, minor))
    scale = jnp.ones_like(largest)
    for power in (64, 32, 16, 8, 4, 2, 1):
        room = largest * (2.0**power) < RADIX
        largest = jnp.where(room, largest * (2.0**power), largest)
        scale = jnp.where(room, scale * (2.0**power), scale)
    for power in (2, 1):
        over = largest >= RADIX
        largest = jnp.where(over, largest * (0.5**power), largest)
        scale = jnp.where(over, scale * (0.5**power), scale)
    scale_ref[...] = scale

    def split(row, _):
        rest = held[row] * scale
        digits = []
        for _ in range(DIGITS):
            digit = jnp.round(rest)
            digits.append(digit)
            rest = (rest - digit) * RADIX
        out_ref[:, pl.ds(pl.multiple_of(row * minor, minor), minor)] = jnp.concatenate(digits, axis=0).astype(FP8)
        return 0

    lax.fori_loop(0, major, split, 0, unroll=8)


def scaled_direction(gradient, first, second, rows):
    sequences, major, minor = gradient.shape
    return pl.pallas_call(
        functools.partial(direction_kernel, rows),
        out_shape=(
            jax.ShapeDtypeStruct((DIGITS * sequences, major * minor), FP8),
            jax.ShapeDtypeStruct((sequences, minor), jnp.float32),
        ),
        scratch_shapes=[
            pltpu.VMEM((major, sequences, minor), jnp.float32),
            pltpu.VMEM((major, minor), jnp.float32),
            pltpu.VMEM((major, minor), jnp.float32),
        ],
        compiler_params=pltpu.CompilerParams(vmem_limit_bytes=24 << 20),
        cost_estimate=pl.CostEstimate(
            flops=20 * gradient.size, bytes_accessed=5 * gradient.size, transcendentals=2 * gradient.size
        ),
        name="direction",
    )(gradient, first, second)


def project_kernel(rows, groups, rank, final_scale, seed_ref, direction_ref, scale_ref, kept_ref, out_ref, total, *tiles):
    tile, step = pl.program_id(0), pl.program_id(1)
    sequences = scale_ref.shape[0]
    start = step_start(rows, rank, groups, step)
    last_rows = TILES[-1]

    def multiply(at, signs):
        at = pl.ds(pl.multiple_of(at, 256), signs.shape[0])
        total[...] += jnp.dot(direction_ref[:, at], signs[...], preferred_element_type=jnp.float32)

    @pl.when(step == 0)
    def _():
        total[...] = jnp.zeros_like(total)
        tiles[-1][...] = jnp.zeros_like(tiles[-1])

    here = step * STEP_ROWS
    offset = KEPT_ROWS
    base = hash_base(seed_ref, tile, start, strides(rows, rank)[1])
    for index, count in enumerate(TILES):
        write_signs(base, rows, rank, offset, count, tiles[index])
        if index == 0:
            multiply(jnp.maximum(here - last_rows, 0), tiles[-1])
            multiply(here, kept_ref)
        else:
            multiply(here + offset - TILES[index - 1], tiles[index - 1])
        offset += count

    @pl.when(step == pl.num_programs(1) - 1)
    def _():
        multiply(here + STEP_ROWS - last_rows, tiles[-1])
        inverse = (1.0 / scale_ref[...])[:, :1]
        value = total[(DIGITS - 1) * sequences :, :]
        for digit in reversed(range(DIGITS - 1)):
            value = total[digit * sequences : (digit + 1) * sequences, :] + value * (1.0 / RADIX)
        value = value * inverse * final_scale
        for sequence in range(sequences):
            out_ref[0, sequence] = value[sequence : sequence + 1, :]


def project(seeds, direction, scale, kept, rows, groups, rank, final_scale):
    features = seeds.shape[0] * FEAT_BLOCK
    sequences = scale.shape[0]
    params = rows * rank
    steps = params // STEP_ROWS
    return pl.pallas_call(
        functools.partial(project_kernel, rows, groups, rank, final_scale),
        grid=(features // TILE_FEATS, steps),
        in_specs=[
            pl.BlockSpec(memory_space=pltpu.SMEM),
            pl.BlockSpec((DIGITS * sequences, params), lambda tile, step: (0, 0)),
            pl.BlockSpec(scale.shape, lambda tile, step: (0, 0)),
            pl.BlockSpec((KEPT_ROWS, TILE_FEATS), lambda tile, step: (step, tile)),
        ],
        out_specs=pl.BlockSpec((1, sequences, 1, TILE_FEATS), lambda tile, step: (tile, 0, 0, 0)),
        out_shape=jax.ShapeDtypeStruct((features // TILE_FEATS, sequences, 1, TILE_FEATS), jnp.float32),
        scratch_shapes=[pltpu.VMEM((DIGITS * sequences, TILE_FEATS), jnp.float32)]
        + [pltpu.VMEM((count, TILE_FEATS), FP8) for count in TILES],
        compiler_params=pltpu.CompilerParams(vmem_limit_bytes=32 << 20),
        cost_estimate=pl.CostEstimate(
            flops=10 * params * features, bytes_accessed=params * features // 4, transcendentals=0
        ),
        name="project",
    )(seeds, direction, scale, kept)


def local(
    hidden_input_rows,
    rank_cotangent,
    token_identifiers,
    adam_first_moment,
    adam_second_moment,
    block_seeds,
):
    groups, device_list = lax.axis_size("groups"), lax.axis_size("dp")
    hidden_width = hidden_input_rows.shape[1]
    rank = rank_cotangent.shape[1]
    rows = adam_first_moment.shape[0] // groups
    half = device_list // 2
    core = lax.axis_index("dp") & 1
    blocks = rows * rank // STEP_ROWS * (block_seeds.shape[0] * FEAT_BLOCK // TILE_FEATS)
    early = min(EARLY_BLOCKS, blocks // 2)
    held = (rank_cotangent, token_identifiers)

    given = half_gradient(hidden_input_rows, *held, 1 - core, groups, rows)
    pairs = [(source, source ^ 1) for source in range(device_list)]
    other = lax.ppermute(given, "dp", pairs)
    kept = kept_signs(block_seeds, rows, groups, rank, 0, early, given, False)
    summed = half_gradient(hidden_input_rows, *held, core, groups, rows, other, kept)
    everyone = [
        [group * device_list + 2 * pair + side for group in range(groups) for pair in range(half)]
        for side in range(2)
    ]
    summed = summed.reshape((groups * half,) + summed.shape[2:])
    gradient = lax.all_to_all(
        summed, ("groups", "dp"), split_axis=0, concat_axis=0, axis_index_groups=everyone, tiled=True
    )
    kept = kept_signs(block_seeds, rows, groups, rank, early, blocks - early, kept, True)
    direction, scale = scaled_direction(gradient, adam_first_moment, adam_second_moment, rows)
    final_scale = 1.0 / math.sqrt(hidden_width * rank)
    partial = project(block_seeds, direction, scale, kept, rows, groups, rank, final_scale)
    partial = partial.reshape((groups * device_list, 1, TILE_FEATS))
    by_half = [
        group * device_list + 2 * pair + side for side in range(2) for group in range(groups) for pair in range(half)
    ]
    partial = lax.all_to_all(
        partial, ("groups", "dp"), split_axis=0, concat_axis=0, axis_index_groups=[by_half], tiled=True
    )
    return jnp.sum(partial, axis=0)


def solution(mesh):
    in_specs = (
        P(("groups", "dp"), None),
        P(("groups", "dp"), None),
        P(("groups", "dp")),
        P("dp", None),
        P("dp", None),
        P(),
    )
    out_specs = P(("groups", "dp"), None)
    return jax.shard_map(local, mesh=mesh, in_specs=in_specs, out_specs=out_specs, check_vma=False)
```

```python
import functools
import math

import jax
import jax.numpy as jnp
from jax import lax
from jax.experimental import pallas as pl
from jax.experimental.pallas import tpu as pltpu
from jax.sharding import PartitionSpec as P

FEAT_BLOCK = 512
beta_one = 0.9
beta_two = 0.999
epsilon = 1e-08
mix_feature = 1640531527
mix_param = 2028178513
mix_round = 73244475
DIGITS = 4
RADIX = 16.0
FP8 = jnp.float8_e4m3fn
STEP_ROWS = 4096
KEPT_ROWS = 1536
KEPT_BLOCK = 512
TILES = (1024, 1024, 512)
EARLY_BLOCKS = 4
TILE_FEATS = 2048


def wrap(value):
    value &= 0xFFFFFFFF
    return jnp.int32(value - (1 << 32) if value >= (1 << 31) else value)


def scramble(hashed):
    hashed = hashed ^ lax.shift_right_logical(hashed, jnp.full_like(hashed, 16))
    hashed = hashed * mix_round
    hashed = hashed ^ lax.shift_right_logical(hashed, jnp.full_like(hashed, 16))
    return hashed * mix_round


def strides(rows, rank):
    return (1, rank) if rows % 128 == 0 else (rank, 1)


def minor_size(rows, rank):
    return rows if rows % 128 == 0 else rank


def step_start(rows, rank, groups, step):
    mine = lax.axis_index("dp") * groups + lax.axis_index("groups")
    return mine * (rows * rank) + step * (STEP_ROWS // minor_size(rows, rank) * strides(rows, rank)[0])


def hash_base(seed_ref, feature_tile, start, minor_stride):
    pieces = []
    for piece in range(TILE_FEATS // FEAT_BLOCK):
        block = feature_tile * (TILE_FEATS // FEAT_BLOCK) + piece
        down = lax.broadcasted_iota(jnp.int32, (8, FEAT_BLOCK), 0)
        across = lax.broadcasted_iota(jnp.int32, (8, FEAT_BLOCK), 1)
        scalar = seed_ref[block] + block * wrap(FEAT_BLOCK * mix_feature) + start * wrap(mix_param)
        pieces.append(down * wrap(mix_param * minor_stride) + across * wrap(mix_feature) + scalar)
    return jnp.concatenate(pieces, axis=1)


def write_signs(base, rows, rank, offset, count, out_ref):
    minor, (major_stride, minor_stride) = minor_size(rows, rank), strides(rows, rank)
    for top in range(0, count, 32):
        hashes = []
        for part in range(offset + top, offset + top + 32, 8):
            apart = part // minor * major_stride + part % minor * minor_stride
            hashes.append(scramble(base + wrap(mix_param * apart)))
        hashed = jnp.concatenate(hashes, axis=0)
        out_ref[pl.ds(top, 32), :] = jnp.where(hashed < 0, FP8(-1), FP8(1))


def gradient_kernel(away, inputs_ref, cotangent_ref, tokens_ref, *refs):
    *other_refs, out_ref, inputs, cotangent, tokens, result, sems, out_sems = refs
    groups, pairs, _, rows = out_ref.shape
    width = groups * rows
    side = lax.axis_index("dp") & 1
    side = 1 - side if away else side
    small = [
        pltpu.make_async_copy(cotangent_ref, cotangent, sems.at[pairs]),
        pltpu.make_async_copy(tokens_ref, tokens, sems.at[pairs + 1]),
    ]
    large = []
    for pair in range(pairs):
        columns = pl.ds(pl.multiple_of((2 * pair + side) * width, 128), width)
        large.append(pltpu.make_async_copy(inputs_ref.at[:, columns], inputs.at[pair], sems.at[pair]))
    for copy in small + large:
        copy.start()
    for copy in small:
        copy.wait()
    turned = cotangent[...].astype(jnp.float32).T
    masked = jnp.where(tokens[...] != 0, turned, 0.0).astype(jnp.bfloat16)
    copies = []
    for pair in range(pairs):
        large[pair].wait()
        part = jnp.dot(masked, inputs[pair], preferred_element_type=jnp.float32)
        for group in range(groups):
            piece = part[:, group * rows : (group + 1) * rows]
            if other_refs:
                piece = piece + other_refs[0][group, pair]
            result[group, pair] = piece
            copies.append(
                pltpu.make_async_copy(
                    result.at[group, pair], out_ref.at[group, pair], out_sems.at[group, pair]
                )
            )
            copies[-1].start()
    for copy in copies:
        copy.wait()


def half_gradient(inputs, cotangent, tokens, away, groups, rows, other=None, after=None):
    count, width = inputs.shape
    rank = cotangent.shape[1]
    pairs = width // (2 * groups * rows)
    if rows % 128:
        side = lax.axis_index("dp") & 1
        side = 1 - side if away else side
        masked = jnp.where((tokens != 0)[:, None], cotangent, jnp.bfloat16(0))
        whole = lax.dot_general(
            inputs, masked, (((0,), (0,)), ((), ())), preferred_element_type=jnp.float32
        )
        whole = whole.reshape(pairs, 2, groups, rows, rank)
        mine = lax.dynamic_index_in_dim(whole, side, 1, keepdims=False).swapaxes(0, 1)
        if other is None:
            return mine
        other, _ = lax.optimization_barrier((other, after))
        return mine + other
    in_specs = [pl.BlockSpec(memory_space=pltpu.HBM)] * 3
    operands = [inputs, cotangent, tokens[None, :]]
    if other is not None:
        in_specs += [pl.BlockSpec(memory_space=pltpu.VMEM), pl.BlockSpec(memory_space=pl.ANY)]
        operands += [other, after]
    return pl.pallas_call(
        functools.partial(gradient_kernel, away),
        in_specs=in_specs,
        out_specs=pl.BlockSpec(memory_space=pl.ANY),
        out_shape=jax.ShapeDtypeStruct((groups, pairs, rank, rows), jnp.float32),
        scratch_shapes=[
            pltpu.VMEM((pairs, count, groups * rows), jnp.bfloat16),
            pltpu.VMEM((count, rank), jnp.bfloat16),
            pltpu.VMEM((1, count), jnp.int32),
            pltpu.VMEM((groups, pairs, rank, rows), jnp.float32),
            pltpu.SemaphoreType.DMA((pairs + 2,)),
            pltpu.SemaphoreType.DMA((groups, pairs)),
        ],
        compiler_params=pltpu.CompilerParams(vmem_limit_bytes=None if other is None else 12 << 20),
        cost_estimate=pl.CostEstimate(
            flops=count * width * rank, bytes_accessed=count * width + 4 * width * rank, transcendentals=0
        ),
        name="half_gradient",
    )(*operands)


def signs_kernel(rows, groups, rank, first, seed_ref, *refs):
    block = first + pl.program_id(0)
    tiles = seed_ref.shape[0] * FEAT_BLOCK // TILE_FEATS
    part = block // tiles
    apart = KEPT_ROWS // KEPT_BLOCK
    start = step_start(rows, rank, groups, part // apart)
    start += part % apart * (KEPT_BLOCK // minor_size(rows, rank) * strides(rows, rank)[0])
    base = hash_base(seed_ref, block % tiles, start, strides(rows, rank)[1])
    write_signs(base, rows, rank, 0, KEPT_BLOCK, refs[-1])


def kept_signs(seeds, rows, groups, rank, first, count, after, alias):
    features = seeds.shape[0] * FEAT_BLOCK
    steps, tiles = rows * rank // STEP_ROWS, features // TILE_FEATS
    size = count * KEPT_BLOCK * TILE_FEATS
    return pl.pallas_call(
        functools.partial(signs_kernel, rows, groups, rank, first),
        grid=(count,),
        in_specs=[pl.BlockSpec(memory_space=pltpu.SMEM), pl.BlockSpec(memory_space=pl.ANY)],
        out_specs=pl.BlockSpec(
            (KEPT_BLOCK, TILE_FEATS), lambda index: ((index + first) // tiles, (index + first) % tiles)
        ),
        out_shape=jax.ShapeDtypeStruct((steps * KEPT_ROWS, features), FP8),
        input_output_aliases={1: 0} if alias else {},
        compiler_params=pltpu.CompilerParams(vmem_limit_bytes=16 << 20),
        cost_estimate=pl.CostEstimate(flops=size * 10, bytes_accessed=size, transcendentals=0),
        name="kept_signs",
    )(seeds, after)


def direction_kernel(rows, gradient_ref, first_ref, second_ref, out_ref, scale_ref, held, first, second):
    sequences, major, minor = gradient_ref.shape
    mine = pl.ds(pl.multiple_of(lax.axis_index("groups") * rows, 8), rows)
    turn = major != rows
    first[...] = first_ref[mine, :].T if turn else first_ref[mine, :]
    second[...] = second_ref[mine, :].T if turn else second_ref[mine, :]

    def moments(block, largest):
        at = pl.ds(pl.multiple_of(block * 8, 8), 8)
        gradient = gradient_ref[:, at, :]
        moment_one = beta_one * first[at, :][None] + (1 - beta_one) * gradient
        moment_two = beta_two * second[at, :][None] + (1 - beta_two) * gradient * gradient
        direction = moment_one / (jnp.sqrt(moment_two) + epsilon)
        direction = direction.astype(jnp.bfloat16).astype(jnp.float32)
        direction = jnp.swapaxes(direction, 0, 1)
        for row in range(8):
            held[block * 8 + row] = direction[row]
        return jnp.maximum(largest, jnp.max(jnp.abs(direction), axis=0))

    largest = lax.fori_loop(0, major // 8, moments, jnp.zeros((sequences, minor), jnp.float32))
    largest = jnp.broadcast_to(jnp.max(largest, axis=1, keepdims=True), (sequences, minor))
    scale = jnp.ones_like(largest)
    for power in (64, 32, 16, 8, 4, 2, 1):
        room = largest * (2.0**power) < RADIX
        largest = jnp.where(room, largest * (2.0**power), largest)
        scale = jnp.where(room, scale * (2.0**power), scale)
    for power in (2, 1):
        over = largest >= RADIX
        largest = jnp.where(over, largest * (0.5**power), largest)
        scale = jnp.where(over, scale * (0.5**power), scale)
    scale_ref[...] = scale

    def split(row, _):
        rest = held[row] * scale
        digits = []
        for _ in range(DIGITS):
            digit = jnp.round(rest)
            digits.append(digit)
            rest = (rest - digit) * RADIX
        out_ref[:, pl.ds(pl.multiple_of(row * minor, minor), minor)] = jnp.concatenate(digits, axis=0).astype(FP8)
        return 0

    lax.fori_loop(0, major, split, 0, unroll=8)


def scaled_direction(gradient, first, second, rows):
    sequences, major, minor = gradient.shape
    return pl.pallas_call(
        functools.partial(direction_kernel, rows),
        out_shape=(
            jax.ShapeDtypeStruct((DIGITS * sequences, major * minor), FP8),
            jax.ShapeDtypeStruct((sequences, minor), jnp.float32),
        ),
        scratch_shapes=[
            pltpu.VMEM((major, sequences, minor), jnp.float32),
            pltpu.VMEM((major, minor), jnp.float32),
            pltpu.VMEM((major, minor), jnp.float32),
        ],
        compiler_params=pltpu.CompilerParams(vmem_limit_bytes=24 << 20),
        cost_estimate=pl.CostEstimate(
            flops=20 * gradient.size, bytes_accessed=5 * gradient.size, transcendentals=2 * gradient.size
        ),
        name="direction",
    )(gradient, first, second)


def project_kernel(rows, groups, rank, final_scale, seed_ref, direction_ref, scale_ref, kept_ref, out_ref, total, *tiles):
    tile, step = pl.program_id(0), pl.program_id(1)
    sequences = scale_ref.shape[0]
    start = step_start(rows, rank, groups, step)
    last_rows = TILES[-1]

    def multiply(at, signs):
        at = pl.ds(pl.multiple_of(at, 256), signs.shape[0])
        total[...] += jnp.dot(direction_ref[:, at], signs[...], preferred_element_type=jnp.float32)

    @pl.when(step == 0)
    def _():
        total[...] = jnp.zeros_like(total)
        tiles[-1][...] = jnp.zeros_like(tiles[-1])

    here = step * STEP_ROWS
    offset = KEPT_ROWS
    base = hash_base(seed_ref, tile, start, strides(rows, rank)[1])
    for index, count in enumerate(TILES):
        write_signs(base, rows, rank, offset, count, tiles[index])
        if index == 0:
            multiply(jnp.maximum(here - last_rows, 0), tiles[-1])
            multiply(here, kept_ref)
        else:
            multiply(here + offset - TILES[index - 1], tiles[index - 1])
        offset += count

    @pl.when(step == pl.num_programs(1) - 1)
    def _():
        multiply(here + STEP_ROWS - last_rows, tiles[-1])
        inverse = (1.0 / scale_ref[...])[:, :1]
        value = total[(DIGITS - 1) * sequences :, :]
        for digit in reversed(range(DIGITS - 1)):
            value = total[digit * sequences : (digit + 1) * sequences, :] + value * (1.0 / RADIX)
        value = value * inverse * final_scale
        for sequence in range(sequences):
            out_ref[0, sequence] = value[sequence : sequence + 1, :]


def project(seeds, direction, scale, kept, rows, groups, rank, final_scale):
    features = seeds.shape[0] * FEAT_BLOCK
    sequences = scale.shape[0]
    params = rows * rank
    steps = params // STEP_ROWS
    return pl.pallas_call(
        functools.partial(project_kernel, rows, groups, rank, final_scale),
        grid=(features // TILE_FEATS, steps),
        in_specs=[
            pl.BlockSpec(memory_space=pltpu.SMEM),
            pl.BlockSpec((DIGITS * sequences, params), lambda tile, step: (0, 0)),
            pl.BlockSpec(scale.shape, lambda tile, step: (0, 0)),
            pl.BlockSpec((KEPT_ROWS, TILE_FEATS), lambda tile, step: (step, tile)),
        ],
        out_specs=pl.BlockSpec((1, sequences, 1, TILE_FEATS), lambda tile, step: (tile, 0, 0, 0)),
        out_shape=jax.ShapeDtypeStruct((features // TILE_FEATS, sequences, 1, TILE_FEATS), jnp.float32),
        scratch_shapes=[pltpu.VMEM((DIGITS * sequences, TILE_FEATS), jnp.float32)]
        + [pltpu.VMEM((count, TILE_FEATS), FP8) for count in TILES],
        compiler_params=pltpu.CompilerParams(vmem_limit_bytes=32 << 20),
        cost_estimate=pl.CostEstimate(
            flops=10 * params * features, bytes_accessed=params * features // 4, transcendentals=0
        ),
        name="project",
    )(seeds, direction, scale, kept)


def local(
    hidden_input_rows,
    rank_cotangent,
    token_identifiers,
    adam_first_moment,
    adam_second_moment,
    block_seeds,
):
    groups, device_list = lax.axis_size("groups"), lax.axis_size("dp")
    hidden_width = hidden_input_rows.shape[1]
    rank = rank_cotangent.shape[1]
    rows = adam_first_moment.shape[0] // groups
    half = device_list // 2
    kept_rows = rows * rank // STEP_ROWS * KEPT_ROWS
    blocks = kept_rows // KEPT_BLOCK * (block_seeds.shape[0] * FEAT_BLOCK // TILE_FEATS)
    early = min(EARLY_BLOCKS, blocks // 2)
    held = (rank_cotangent, token_identifiers)

    given = half_gradient(hidden_input_rows, *held, True, groups, rows)
    pairs = [(source, source ^ 1) for source in range(device_list)]
    other = lax.ppermute(given, "dp", pairs)
    kept = kept_signs(block_seeds, rows, groups, rank, 0, early, given, False)
    summed = half_gradient(hidden_input_rows, *held, False, groups, rows, other, kept)
    everyone = [
        [group * device_list + 2 * pair + side for group in range(groups) for pair in range(half)]
        for side in range(2)
    ]
    summed = summed.reshape((groups * half,) + summed.shape[2:])
    gradient = lax.all_to_all(
        summed, ("groups", "dp"), split_axis=0, concat_axis=0, axis_index_groups=everyone, tiled=True
    )
    kept = kept_signs(block_seeds, rows, groups, rank, early, blocks - early, kept, True)
    direction, scale = scaled_direction(gradient, adam_first_moment, adam_second_moment, rows)
    final_scale = 1.0 / math.sqrt(hidden_width * rank)
    partial = project(block_seeds, direction, scale, kept, rows, groups, rank, final_scale)
    partial = partial.reshape((groups * device_list, 1, TILE_FEATS))
    by_half = [
        group * device_list + 2 * pair + side for side in range(2) for group in range(groups) for pair in range(half)
    ]
    partial = lax.all_to_all(
        partial, ("groups", "dp"), split_axis=0, concat_axis=0, axis_index_groups=[by_half], tiled=True
    )
    return jnp.sum(partial, axis=0)


def solution(mesh):
    in_specs = (
        P(("groups", "dp"), None),
        P(("groups", "dp"), None),
        P(("groups", "dp")),
        P("dp", None),
        P("dp", None),
        P(),
    )
    out_specs = P(("groups", "dp"), None)
    return jax.shard_map(local, mesh=mesh, in_specs=in_specs, out_specs=out_specs, check_vma=False)
```

```python
import functools
import math

import jax
import jax.numpy as jnp
from jax import lax
from jax.experimental import pallas as pl
from jax.experimental.pallas import tpu as pltpu
from jax.sharding import PartitionSpec as P

FEAT_BLOCK = 512
beta_one = 0.9
beta_two = 0.999
epsilon = 1e-08
mix_feature = 1640531527
mix_param = 2028178513
mix_round = 73244475
DIGITS = 4
RADIX = 16.0
FP8 = jnp.float8_e4m3fn
STEP_ROWS = 4096
KEPT_ROWS = 1536
KEPT_BLOCK = 768
TILES = (1280, 1024, 256)
EARLY_BLOCKS = 3
TILE_FEATS = 2048


def wrap(value):
    value &= 0xFFFFFFFF
    return jnp.int32(value - (1 << 32) if value >= (1 << 31) else value)


def scramble(hashed):
    hashed = hashed ^ lax.shift_right_logical(hashed, jnp.full_like(hashed, 16))
    hashed = hashed * mix_round
    hashed = hashed ^ lax.shift_right_logical(hashed, jnp.full_like(hashed, 16))
    return hashed * mix_round


def strides(rows, rank):
    return (1, rank) if rows % 128 == 0 else (rank, 1)


def minor_size(rows, rank):
    return rows if rows % 128 == 0 else rank


def step_start(rows, rank, groups, step):
    mine = lax.axis_index("dp") * groups + lax.axis_index("groups")
    return mine * (rows * rank) + step * (STEP_ROWS // minor_size(rows, rank) * strides(rows, rank)[0])


def hash_base(seed_ref, feature_tile, start, minor_stride):
    pieces = []
    for piece in range(TILE_FEATS // FEAT_BLOCK):
        block = feature_tile * (TILE_FEATS // FEAT_BLOCK) + piece
        down = lax.broadcasted_iota(jnp.int32, (8, FEAT_BLOCK), 0)
        across = lax.broadcasted_iota(jnp.int32, (8, FEAT_BLOCK), 1)
        scalar = seed_ref[block] + block * wrap(FEAT_BLOCK * mix_feature) + start * wrap(mix_param)
        pieces.append(down * wrap(mix_param * minor_stride) + across * wrap(mix_feature) + scalar)
    return jnp.concatenate(pieces, axis=1)


def write_signs(base, rows, rank, offset, count, out_ref):
    minor, (major_stride, minor_stride) = minor_size(rows, rank), strides(rows, rank)
    for top in range(0, count, 32):
        hashes = []
        for part in range(offset + top, offset + top + 32, 8):
            apart = part // minor * major_stride + part % minor * minor_stride
            hashes.append(scramble(base + wrap(mix_param * apart)))
        hashed = jnp.concatenate(hashes, axis=0)
        out_ref[pl.ds(top, 32), :] = jnp.where(hashed < 0, FP8(-1), FP8(1))


def gradient_kernel(away, inputs_ref, cotangent_ref, tokens_ref, *refs):
    *ends, inputs, cotangent, tokens, result, sems, out_sems = refs
    if away:
        out_ref, token_ref = ends
        other_ref = None
        token_ref[0] = 0
    else:
        other_ref, _, out_ref = ends
    groups, pairs, _, rows = out_ref.shape
    width = groups * rows
    side = lax.axis_index("dp") & 1
    side = 1 - side if away else side
    small = [
        pltpu.make_async_copy(cotangent_ref, cotangent, sems.at[pairs]),
        pltpu.make_async_copy(tokens_ref, tokens, sems.at[pairs + 1]),
    ]
    large = []
    for pair in range(pairs):
        columns = pl.ds(pl.multiple_of((2 * pair + side) * width, 128), width)
        large.append(pltpu.make_async_copy(inputs_ref.at[:, columns], inputs.at[pair], sems.at[pair]))
    for copy in small + large:
        copy.start()
    for copy in small:
        copy.wait()
    turned = cotangent[...].astype(jnp.float32).T
    masked = jnp.where(tokens[...] != 0, turned, 0.0).astype(jnp.bfloat16)
    copies = []
    for pair in range(pairs):
        large[pair].wait()
        part = jnp.dot(masked, inputs[pair], preferred_element_type=jnp.float32)
        for group in range(groups):
            piece = part[:, group * rows : (group + 1) * rows]
            if other_ref is not None:
                piece = piece + other_ref[group, pair]
            result[group, pair] = piece
            copies.append(
                pltpu.make_async_copy(
                    result.at[group, pair], out_ref.at[group, pair], out_sems.at[group, pair]
                )
            )
            copies[-1].start()
    for copy in copies:
        copy.wait()


def half_gradient(inputs, cotangent, tokens, away, groups, rows, other=None, after=None):
    count, width = inputs.shape
    rank = cotangent.shape[1]
    pairs = width // (2 * groups * rows)
    if rows % 128:
        side = lax.axis_index("dp") & 1
        side = 1 - side if away else side
        masked = jnp.where((tokens != 0)[:, None], cotangent, jnp.bfloat16(0))
        whole = lax.dot_general(
            inputs, masked, (((0,), (0,)), ((), ())), preferred_element_type=jnp.float32
        )
        whole = whole.reshape(pairs, 2, groups, rows, rank)
        mine = lax.dynamic_index_in_dim(whole, side, 1, keepdims=False).swapaxes(0, 1)
        if away:
            return mine, jnp.zeros((1,), jnp.int32)
        other, _ = lax.optimization_barrier((other, after))
        return mine + other
    in_specs = [pl.BlockSpec(memory_space=pltpu.HBM)] * 3
    operands = [inputs, cotangent, tokens[None, :]]
    out_specs = pl.BlockSpec(memory_space=pl.ANY)
    out_shape = jax.ShapeDtypeStruct((groups, pairs, rank, rows), jnp.float32)
    if away:
        out_specs = (out_specs, pl.BlockSpec(memory_space=pltpu.SMEM))
        out_shape = (out_shape, jax.ShapeDtypeStruct((1,), jnp.int32))
    else:
        in_specs += [pl.BlockSpec(memory_space=pltpu.VMEM), pl.BlockSpec(memory_space=pl.ANY)]
        operands += [other, after]
    return pl.pallas_call(
        functools.partial(gradient_kernel, away),
        in_specs=in_specs,
        out_specs=out_specs,
        out_shape=out_shape,
        scratch_shapes=[
            pltpu.VMEM((pairs, count, groups * rows), jnp.bfloat16),
            pltpu.VMEM((count, rank), jnp.bfloat16),
            pltpu.VMEM((1, count), jnp.int32),
            pltpu.VMEM((groups, pairs, rank, rows), jnp.float32),
            pltpu.SemaphoreType.DMA((pairs + 2,)),
            pltpu.SemaphoreType.DMA((groups, pairs)),
        ],
        compiler_params=pltpu.CompilerParams(vmem_limit_bytes=None if away else 12 << 20),
        cost_estimate=pl.CostEstimate(
            flops=count * width * rank, bytes_accessed=count * width + 4 * width * rank, transcendentals=0
        ),
        name="half_gradient",
    )(*operands)


def signs_kernel(rows, groups, rank, first, seed_ref, *refs):
    block = first + pl.program_id(0)
    tiles = seed_ref.shape[0] * FEAT_BLOCK // TILE_FEATS
    part = block // tiles
    apart = KEPT_ROWS // KEPT_BLOCK
    start = step_start(rows, rank, groups, part // apart)
    start += part % apart * (KEPT_BLOCK // minor_size(rows, rank) * strides(rows, rank)[0])
    base = hash_base(seed_ref, block % tiles, start, strides(rows, rank)[1])
    write_signs(base, rows, rank, 0, KEPT_BLOCK, refs[-1])


def kept_signs(seeds, rows, groups, rank, first, count, after, alias):
    features = seeds.shape[0] * FEAT_BLOCK
    steps, tiles = rows * rank // STEP_ROWS, features // TILE_FEATS
    size = count * KEPT_BLOCK * TILE_FEATS
    return pl.pallas_call(
        functools.partial(signs_kernel, rows, groups, rank, first),
        grid=(count,),
        in_specs=[pl.BlockSpec(memory_space=pltpu.SMEM)]
        + [pl.BlockSpec(memory_space=pl.ANY if alias else pltpu.SMEM)],
        out_specs=pl.BlockSpec(
            (KEPT_BLOCK, TILE_FEATS), lambda index: ((index + first) // tiles, (index + first) % tiles)
        ),
        out_shape=jax.ShapeDtypeStruct((steps * KEPT_ROWS, features), FP8),
        input_output_aliases={1: 0} if alias else {},
        compiler_params=pltpu.CompilerParams(vmem_limit_bytes=16 << 20),
        cost_estimate=pl.CostEstimate(flops=size * 10, bytes_accessed=size, transcendentals=0),
        name="kept_signs",
    )(seeds, after)


def direction_kernel(rows, gradient_ref, first_ref, second_ref, out_ref, scale_ref, held, first, second):
    sequences, major, minor = gradient_ref.shape
    mine = pl.ds(pl.multiple_of(lax.axis_index("groups") * rows, 8), rows)
    turn = major != rows
    first[...] = first_ref[mine, :].T if turn else first_ref[mine, :]
    second[...] = second_ref[mine, :].T if turn else second_ref[mine, :]

    def moments(block, largest):
        at = pl.ds(pl.multiple_of(block * 8, 8), 8)
        gradient = gradient_ref[:, at, :]
        moment_one = beta_one * first[at, :][None] + (1 - beta_one) * gradient
        moment_two = beta_two * second[at, :][None] + (1 - beta_two) * gradient * gradient
        direction = moment_one / (moment_two * lax.rsqrt(moment_two) + epsilon)
        direction = direction.astype(jnp.bfloat16).astype(jnp.float32)
        direction = jnp.swapaxes(direction, 0, 1)
        for row in range(8):
            held[block * 8 + row] = direction[row]
        return jnp.maximum(largest, jnp.max(jnp.abs(direction), axis=0))

    largest = lax.fori_loop(0, major // 8, moments, jnp.zeros((sequences, minor), jnp.float32))
    largest = jnp.broadcast_to(jnp.max(largest, axis=1, keepdims=True), (sequences, minor))
    scale = jnp.ones_like(largest)
    for power in (64, 32, 16, 8, 4, 2, 1):
        room = largest * (2.0**power) < RADIX
        largest = jnp.where(room, largest * (2.0**power), largest)
        scale = jnp.where(room, scale * (2.0**power), scale)
    for power in (2, 1):
        over = largest >= RADIX
        largest = jnp.where(over, largest * (0.5**power), largest)
        scale = jnp.where(over, scale * (0.5**power), scale)
    scale_ref[...] = scale

    def split(row, _):
        rest = held[row] * scale
        digits = []
        for _ in range(DIGITS):
            digit = jnp.round(rest)
            digits.append(digit)
            rest = (rest - digit) * RADIX
        out_ref[:, pl.ds(pl.multiple_of(row * minor, minor), minor)] = jnp.concatenate(digits, axis=0).astype(FP8)
        return 0

    lax.fori_loop(0, major, split, 0, unroll=8)


def scaled_direction(gradient, first, second, rows):
    sequences, major, minor = gradient.shape
    return pl.pallas_call(
        functools.partial(direction_kernel, rows),
        out_shape=(
            jax.ShapeDtypeStruct((DIGITS * sequences, major * minor), FP8),
            jax.ShapeDtypeStruct((sequences, minor), jnp.float32),
        ),
        scratch_shapes=[
            pltpu.VMEM((major, sequences, minor), jnp.float32),
            pltpu.VMEM((major, minor), jnp.float32),
            pltpu.VMEM((major, minor), jnp.float32),
        ],
        compiler_params=pltpu.CompilerParams(vmem_limit_bytes=24 << 20),
        cost_estimate=pl.CostEstimate(
            flops=20 * gradient.size, bytes_accessed=5 * gradient.size, transcendentals=2 * gradient.size
        ),
        name="direction",
    )(gradient, first, second)


def project_kernel(rows, groups, rank, final_scale, seed_ref, direction_ref, scale_ref, kept_ref, out_ref, total, *tiles):
    tile, step = pl.program_id(0), pl.program_id(1)
    sequences = scale_ref.shape[0]
    start = step_start(rows, rank, groups, step)
    last_rows = TILES[-1]

    def multiply(at, signs):
        at = pl.ds(pl.multiple_of(at, 256), signs.shape[0])
        total[...] += jnp.dot(direction_ref[:, at], signs[...], preferred_element_type=jnp.float32)

    @pl.when(step == 0)
    def _():
        total[...] = jnp.zeros_like(total)
        tiles[-1][...] = jnp.zeros_like(tiles[-1])

    here = step * STEP_ROWS
    offset = KEPT_ROWS
    base = hash_base(seed_ref, tile, start, strides(rows, rank)[1])
    for index, count in enumerate(TILES):
        write_signs(base, rows, rank, offset, count, tiles[index])
        if index == 0:
            multiply(jnp.maximum(here - last_rows, 0), tiles[-1])
            multiply(here, kept_ref)
        else:
            multiply(here + offset - TILES[index - 1], tiles[index - 1])
        offset += count

    @pl.when(step == pl.num_programs(1) - 1)
    def _():
        multiply(here + STEP_ROWS - last_rows, tiles[-1])
        inverse = (1.0 / scale_ref[...])[:, :1]
        value = total[(DIGITS - 1) * sequences :, :]
        for digit in reversed(range(DIGITS - 1)):
            value = total[digit * sequences : (digit + 1) * sequences, :] + value * (1.0 / RADIX)
        value = value * inverse * final_scale
        for sequence in range(sequences):
            out_ref[0, sequence] = value[sequence : sequence + 1, :]


def project(seeds, direction, scale, kept, rows, groups, rank, final_scale):
    features = seeds.shape[0] * FEAT_BLOCK
    sequences = scale.shape[0]
    params = rows * rank
    steps = params // STEP_ROWS
    return pl.pallas_call(
        functools.partial(project_kernel, rows, groups, rank, final_scale),
        grid=(features // TILE_FEATS, steps),
        in_specs=[
            pl.BlockSpec(memory_space=pltpu.SMEM),
            pl.BlockSpec((DIGITS * sequences, params), lambda tile, step: (0, 0)),
            pl.BlockSpec(scale.shape, lambda tile, step: (0, 0)),
            pl.BlockSpec((KEPT_ROWS, TILE_FEATS), lambda tile, step: (step, tile)),
        ],
        out_specs=pl.BlockSpec((1, sequences, 1, TILE_FEATS), lambda tile, step: (tile, 0, 0, 0)),
        out_shape=jax.ShapeDtypeStruct((features // TILE_FEATS, sequences, 1, TILE_FEATS), jnp.float32),
        scratch_shapes=[pltpu.VMEM((DIGITS * sequences, TILE_FEATS), jnp.float32)]
        + [pltpu.VMEM((count, TILE_FEATS), FP8) for count in TILES],
        compiler_params=pltpu.CompilerParams(vmem_limit_bytes=32 << 20),
        cost_estimate=pl.CostEstimate(
            flops=10 * params * features, bytes_accessed=params * features // 4, transcendentals=0
        ),
        name="project",
    )(seeds, direction, scale, kept)


def local(
    hidden_input_rows,
    rank_cotangent,
    token_identifiers,
    adam_first_moment,
    adam_second_moment,
    block_seeds,
):
    groups, device_list = lax.axis_size("groups"), lax.axis_size("dp")
    hidden_width = hidden_input_rows.shape[1]
    rank = rank_cotangent.shape[1]
    rows = adam_first_moment.shape[0] // groups
    half = device_list // 2
    kept_rows = rows * rank // STEP_ROWS * KEPT_ROWS
    blocks = kept_rows // KEPT_BLOCK * (block_seeds.shape[0] * FEAT_BLOCK // TILE_FEATS)
    early = min(EARLY_BLOCKS, blocks // 2)
    held = (rank_cotangent, token_identifiers)

    given, token = half_gradient(hidden_input_rows, *held, True, groups, rows)
    pairs = [(source, source ^ 1) for source in range(device_list)]
    other = lax.ppermute(given, "dp", pairs)
    kept = kept_signs(block_seeds, rows, groups, rank, 0, early, token, False)
    summed = half_gradient(hidden_input_rows, *held, False, groups, rows, other, kept)
    everyone = [
        [group * device_list + 2 * pair + side for group in range(groups) for pair in range(half)]
        for side in range(2)
    ]
    summed = summed.reshape((groups * half,) + summed.shape[2:])
    gradient = lax.all_to_all(
        summed, ("groups", "dp"), split_axis=0, concat_axis=0, axis_index_groups=everyone, tiled=True
    )
    kept = kept_signs(block_seeds, rows, groups, rank, early, blocks - early, kept, True)
    direction, scale = scaled_direction(gradient, adam_first_moment, adam_second_moment, rows)
    final_scale = 1.0 / math.sqrt(hidden_width * rank)
    partial = project(block_seeds, direction, scale, kept, rows, groups, rank, final_scale)
    partial = partial.reshape((groups * device_list, 1, TILE_FEATS))
    by_half = [
        group * device_list + 2 * pair + side for side in range(2) for group in range(groups) for pair in range(half)
    ]
    partial = lax.all_to_all(
        partial, ("groups", "dp"), split_axis=0, concat_axis=0, axis_index_groups=[by_half], tiled=True
    )
    return jnp.sum(partial, axis=0)


def solution(mesh):
    in_specs = (
        P(("groups", "dp"), None),
        P(("groups", "dp"), None),
        P(("groups", "dp")),
        P("dp", None),
        P("dp", None),
        P(),
    )
    out_specs = P(("groups", "dp"), None)
    return jax.shard_map(local, mesh=mesh, in_specs=in_specs, out_specs=out_specs, check_vma=False)
```

```python
import functools
import math

import jax
import jax.numpy as jnp
from jax import lax
from jax.experimental import pallas as pl
from jax.experimental.pallas import tpu as pltpu
from jax.sharding import PartitionSpec as P

FEAT_BLOCK = 512
beta_one = 0.9
beta_two = 0.999
epsilon = 1e-08
mix_feature = 1640531527
mix_param = 2028178513
mix_round = 73244475
DIGITS = 4
RADIX = 16.0
FP8 = jnp.float8_e4m3fn
STEP_ROWS = 4096
KEPT_ROWS = 1536
TILES = (1280, 1024, 256)
EARLY_ROWS, EARLY_BLOCK = 1024, 256
LATER_BLOCK = 512
TILE_FEATS = 2048


def wrap(value):
    value &= 0xFFFFFFFF
    return jnp.int32(value - (1 << 32) if value >= (1 << 31) else value)


def scramble(hashed):
    hashed = hashed ^ lax.shift_right_logical(hashed, jnp.full_like(hashed, 16))
    hashed = hashed * mix_round
    hashed = hashed ^ lax.shift_right_logical(hashed, jnp.full_like(hashed, 16))
    return hashed * mix_round


def strides(rows, rank):
    return (1, rank) if rows % 128 == 0 else (rank, 1)


def minor_size(rows, rank):
    return rows if rows % 128 == 0 else rank


def step_start(rows, rank, groups, step):
    mine = lax.axis_index("dp") * groups + lax.axis_index("groups")
    return mine * (rows * rank) + step * (STEP_ROWS // minor_size(rows, rank) * strides(rows, rank)[0])


def hash_base(seed_ref, feature_tile, start, minor_stride):
    pieces = []
    for piece in range(TILE_FEATS // FEAT_BLOCK):
        block = feature_tile * (TILE_FEATS // FEAT_BLOCK) + piece
        down = lax.broadcasted_iota(jnp.int32, (8, FEAT_BLOCK), 0)
        across = lax.broadcasted_iota(jnp.int32, (8, FEAT_BLOCK), 1)
        scalar = seed_ref[block] + block * wrap(FEAT_BLOCK * mix_feature) + start * wrap(mix_param)
        pieces.append(down * wrap(mix_param * minor_stride) + across * wrap(mix_feature) + scalar)
    return jnp.concatenate(pieces, axis=1)


def write_signs(base, rows, rank, offset, count, out_ref):
    minor, (major_stride, minor_stride) = minor_size(rows, rank), strides(rows, rank)
    for top in range(0, count, 32):
        hashes = []
        for part in range(offset + top, offset + top + 32, 8):
            apart = part // minor * major_stride + part % minor * minor_stride
            hashes.append(scramble(base + wrap(mix_param * apart)))
        hashed = jnp.concatenate(hashes, axis=0)
        out_ref[pl.ds(top, 32), :] = jnp.where(hashed < 0, FP8(-1), FP8(1))


def gradient_kernel(away, inputs_ref, cotangent_ref, tokens_ref, *refs):
    *ends, inputs, cotangent, tokens, result, sems, out_sems = refs
    other_ref, out_ref = (None, ends[0]) if away else (ends[0], ends[2])
    groups, pairs, _, rows = out_ref.shape
    width = groups * rows
    side = lax.axis_index("dp") & 1
    side = 1 - side if away else side
    small = [
        pltpu.make_async_copy(cotangent_ref, cotangent, sems.at[pairs]),
        pltpu.make_async_copy(tokens_ref, tokens, sems.at[pairs + 1]),
    ]
    large = []
    for pair in range(pairs):
        columns = pl.ds(pl.multiple_of((2 * pair + side) * width, 128), width)
        large.append(pltpu.make_async_copy(inputs_ref.at[:, columns], inputs.at[pair], sems.at[pair]))
    for copy in small + large:
        copy.start()
    for copy in small:
        copy.wait()
    turned = cotangent[...].astype(jnp.float32).T
    masked = jnp.where(tokens[...] != 0, turned, 0.0).astype(jnp.bfloat16)
    copies = []
    for pair in range(pairs):
        large[pair].wait()
        part = jnp.dot(masked, inputs[pair], preferred_element_type=jnp.float32)
        for group in range(groups):
            piece = part[:, group * rows : (group + 1) * rows]
            if other_ref is not None:
                piece = piece + other_ref[group, pair]
            result[group, pair] = piece
            copies.append(
                pltpu.make_async_copy(
                    result.at[group, pair], out_ref.at[group, pair], out_sems.at[group, pair]
                )
            )
            copies[-1].start()
    for copy in copies:
        copy.wait()


def half_gradient(inputs, cotangent, tokens, away, groups, rows, other=None, after=None):
    count, width = inputs.shape
    rank = cotangent.shape[1]
    pairs = width // (2 * groups * rows)
    if rows % 128:
        side = lax.axis_index("dp") & 1
        side = 1 - side if away else side
        masked = jnp.where((tokens != 0)[:, None], cotangent, jnp.bfloat16(0))
        whole = lax.dot_general(
            inputs, masked, (((0,), (0,)), ((), ())), preferred_element_type=jnp.float32
        )
        whole = whole.reshape(pairs, 2, groups, rows, rank)
        mine = lax.dynamic_index_in_dim(whole, side, 1, keepdims=False).swapaxes(0, 1)
        if away:
            return mine
        other, _ = lax.optimization_barrier((other, after))
        return mine + other
    in_specs = [pl.BlockSpec(memory_space=pltpu.HBM)] * 3
    operands = [inputs, cotangent, tokens[None, :]]
    if not away:
        in_specs += [pl.BlockSpec(memory_space=pltpu.VMEM), pl.BlockSpec(memory_space=pl.ANY)]
        operands += [other, after]
    return pl.pallas_call(
        functools.partial(gradient_kernel, away),
        in_specs=in_specs,
        out_specs=pl.BlockSpec(memory_space=pl.ANY),
        out_shape=jax.ShapeDtypeStruct((groups, pairs, rank, rows), jnp.float32),
        scratch_shapes=[
            pltpu.VMEM((pairs, count, groups * rows), jnp.bfloat16),
            pltpu.VMEM((count, rank), jnp.bfloat16),
            pltpu.VMEM((1, count), jnp.int32),
            pltpu.VMEM((groups, pairs, rank, rows), jnp.float32),
            pltpu.SemaphoreType.DMA((pairs + 2,)),
            pltpu.SemaphoreType.DMA((groups, pairs)),
        ],
        compiler_params=pltpu.CompilerParams(vmem_limit_bytes=None if away else 12 << 20),
        cost_estimate=pl.CostEstimate(
            flops=count * width * rank, bytes_accessed=count * width + 4 * width * rank, transcendentals=0
        ),
        name="half_gradient",
    )(*operands)


def signs_kernel(rows, groups, rank, first, seed_ref, *refs):
    out_ref = refs[-1]
    count = out_ref.shape[0]
    tiles = seed_ref.shape[0] * FEAT_BLOCK // TILE_FEATS
    row = first + pl.program_id(0) // tiles * count
    start = step_start(rows, rank, groups, row // KEPT_ROWS)
    start += row % KEPT_ROWS // minor_size(rows, rank) * strides(rows, rank)[0]
    base = hash_base(seed_ref, pl.program_id(0) % tiles, start, strides(rows, rank)[1])
    write_signs(base, rows, rank, 0, count, out_ref)


def kept_signs(seeds, rows, groups, rank, first, last, block, before=None):
    features = seeds.shape[0] * FEAT_BLOCK
    tiles = features // TILE_FEATS
    size = (last - first) * features
    return pl.pallas_call(
        functools.partial(signs_kernel, rows, groups, rank, first),
        grid=((last - first) // block * tiles,),
        in_specs=[pl.BlockSpec(memory_space=pltpu.SMEM)]
        + [pl.BlockSpec(memory_space=pl.ANY)] * (before is not None),
        out_specs=pl.BlockSpec(
            (block, TILE_FEATS), lambda index: (first // block + index // tiles, index % tiles)
        ),
        out_shape=jax.ShapeDtypeStruct((rows * rank // STEP_ROWS * KEPT_ROWS, features), FP8),
        input_output_aliases={} if before is None else {1: 0},
        compiler_params=pltpu.CompilerParams(vmem_limit_bytes=16 << 20),
        cost_estimate=pl.CostEstimate(flops=size * 10, bytes_accessed=size, transcendentals=0),
        name="kept_signs",
    )(seeds, *([] if before is None else [before]))


def direction_kernel(rows, gradient_ref, first_ref, second_ref, out_ref, scale_ref, held, first, second):
    sequences, major, minor = gradient_ref.shape
    mine = pl.ds(pl.multiple_of(lax.axis_index("groups") * rows, 8), rows)
    turn = major != rows
    first[...] = first_ref[mine, :].T if turn else first_ref[mine, :]
    second[...] = second_ref[mine, :].T if turn else second_ref[mine, :]

    def moments(block, largest):
        at = pl.ds(pl.multiple_of(block * 8, 8), 8)
        gradient = gradient_ref[:, at, :]
        moment_one = beta_one * first[at, :][None] + (1 - beta_one) * gradient
        moment_two = beta_two * second[at, :][None] + (1 - beta_two) * gradient * gradient
        direction = moment_one / (moment_two * lax.rsqrt(moment_two) + epsilon)
        direction = direction.astype(jnp.bfloat16).astype(jnp.float32)
        direction = jnp.swapaxes(direction, 0, 1)
        for row in range(8):
            held[block * 8 + row] = direction[row]
        return jnp.maximum(largest, jnp.max(jnp.abs(direction), axis=0))

    largest = lax.fori_loop(0, major // 8, moments, jnp.zeros((sequences, minor), jnp.float32))
    largest = jnp.broadcast_to(jnp.max(largest, axis=1, keepdims=True), (sequences, minor))
    scale = jnp.ones_like(largest)
    for power in (64, 32, 16, 8, 4, 2, 1):
        room = largest * (2.0**power) < RADIX
        largest = jnp.where(room, largest * (2.0**power), largest)
        scale = jnp.where(room, scale * (2.0**power), scale)
    for power in (2, 1):
        over = largest >= RADIX
        largest = jnp.where(over, largest * (0.5**power), largest)
        scale = jnp.where(over, scale * (0.5**power), scale)
    scale_ref[...] = scale

    def split(row, _):
        rest = held[row] * scale
        digits = []
        for _ in range(DIGITS):
            digit = jnp.round(rest)
            digits.append(digit)
            rest = (rest - digit) * RADIX
        out_ref[:, pl.ds(pl.multiple_of(row * minor, minor), minor)] = jnp.concatenate(digits, axis=0).astype(FP8)
        return 0

    lax.fori_loop(0, major, split, 0, unroll=8)


def scaled_direction(gradient, first, second, rows):
    sequences, major, minor = gradient.shape
    return pl.pallas_call(
        functools.partial(direction_kernel, rows),
        out_shape=(
            jax.ShapeDtypeStruct((DIGITS * sequences, major * minor), FP8),
            jax.ShapeDtypeStruct((sequences, minor), jnp.float32),
        ),
        scratch_shapes=[
            pltpu.VMEM((major, sequences, minor), jnp.float32),
            pltpu.VMEM((major, minor), jnp.float32),
            pltpu.VMEM((major, minor), jnp.float32),
        ],
        compiler_params=pltpu.CompilerParams(vmem_limit_bytes=24 << 20),
        cost_estimate=pl.CostEstimate(
            flops=20 * gradient.size, bytes_accessed=5 * gradient.size, transcendentals=2 * gradient.size
        ),
        name="direction",
    )(gradient, first, second)


def project_kernel(rows, groups, rank, final_scale, seed_ref, direction_ref, scale_ref, kept_ref, out_ref, total, *tiles):
    tile, step = pl.program_id(0), pl.program_id(1)
    sequences = scale_ref.shape[0]
    start = step_start(rows, rank, groups, step)
    last_rows = TILES[-1]

    def multiply(at, signs):
        at = pl.ds(pl.multiple_of(at, 256), signs.shape[0])
        total[...] += jnp.dot(direction_ref[:, at], signs[...], preferred_element_type=jnp.float32)

    @pl.when(step == 0)
    def _():
        total[...] = jnp.zeros_like(total)
        tiles[-1][...] = jnp.zeros_like(tiles[-1])

    here = step * STEP_ROWS
    offset = KEPT_ROWS
    base = hash_base(seed_ref, tile, start, strides(rows, rank)[1])
    for index, count in enumerate(TILES):
        write_signs(base, rows, rank, offset, count, tiles[index])
        if index == 0:
            multiply(jnp.maximum(here - last_rows, 0), tiles[-1])
            multiply(here, kept_ref)
        else:
            multiply(here + offset - TILES[index - 1], tiles[index - 1])
        offset += count

    @pl.when(step == pl.num_programs(1) - 1)
    def _():
        multiply(here + STEP_ROWS - last_rows, tiles[-1])
        inverse = (1.0 / scale_ref[...])[:, :1]
        value = total[(DIGITS - 1) * sequences :, :]
        for digit in reversed(range(DIGITS - 1)):
            value = total[digit * sequences : (digit + 1) * sequences, :] + value * (1.0 / RADIX)
        value = value * inverse * final_scale
        for sequence in range(sequences):
            out_ref[0, sequence] = value[sequence : sequence + 1, :]


def project(seeds, direction, scale, kept, rows, groups, rank, final_scale):
    features = seeds.shape[0] * FEAT_BLOCK
    sequences = scale.shape[0]
    params = rows * rank
    steps = params // STEP_ROWS
    return pl.pallas_call(
        functools.partial(project_kernel, rows, groups, rank, final_scale),
        grid=(features // TILE_FEATS, steps),
        in_specs=[
            pl.BlockSpec(memory_space=pltpu.SMEM),
            pl.BlockSpec((DIGITS * sequences, params), lambda tile, step: (0, 0)),
            pl.BlockSpec(scale.shape, lambda tile, step: (0, 0)),
            pl.BlockSpec((KEPT_ROWS, TILE_FEATS), lambda tile, step: (step, tile)),
        ],
        out_specs=pl.BlockSpec((1, sequences, 1, TILE_FEATS), lambda tile, step: (tile, 0, 0, 0)),
        out_shape=jax.ShapeDtypeStruct((features // TILE_FEATS, sequences, 1, TILE_FEATS), jnp.float32),
        scratch_shapes=[pltpu.VMEM((DIGITS * sequences, TILE_FEATS), jnp.float32)]
        + [pltpu.VMEM((count, TILE_FEATS), FP8) for count in TILES],
        compiler_params=pltpu.CompilerParams(vmem_limit_bytes=32 << 20),
        cost_estimate=pl.CostEstimate(
            flops=10 * params * features, bytes_accessed=params * features // 4, transcendentals=0
        ),
        name="project",
    )(seeds, direction, scale, kept)


def local(
    hidden_input_rows,
    rank_cotangent,
    token_identifiers,
    adam_first_moment,
    adam_second_moment,
    block_seeds,
):
    groups, device_list = lax.axis_size("groups"), lax.axis_size("dp")
    hidden_width = hidden_input_rows.shape[1]
    rank = rank_cotangent.shape[1]
    rows = adam_first_moment.shape[0] // groups
    half = device_list // 2
    kept_rows = rows * rank // STEP_ROWS * KEPT_ROWS
    early = min(EARLY_ROWS, kept_rows // 3)
    held = (rank_cotangent, token_identifiers)

    given = half_gradient(hidden_input_rows, *held, True, groups, rows)
    pairs = [(source, source ^ 1) for source in range(device_list)]
    other = lax.ppermute(given, "dp", pairs)
    kept = kept_signs(block_seeds, rows, groups, rank, 0, early, EARLY_BLOCK)
    summed = half_gradient(hidden_input_rows, *held, False, groups, rows, other, kept)
    everyone = [
        [group * device_list + 2 * pair + side for group in range(groups) for pair in range(half)]
        for side in range(2)
    ]
    summed = summed.reshape((groups * half,) + summed.shape[2:])
    gradient = lax.all_to_all(
        summed, ("groups", "dp"), split_axis=0, concat_axis=0, axis_index_groups=everyone, tiled=True
    )
    kept = kept_signs(block_seeds, rows, groups, rank, early, kept_rows, LATER_BLOCK, kept)
    direction, scale = scaled_direction(gradient, adam_first_moment, adam_second_moment, rows)
    final_scale = 1.0 / math.sqrt(hidden_width * rank)
    partial = project(block_seeds, direction, scale, kept, rows, groups, rank, final_scale)
    partial = partial.reshape((groups * device_list, 1, TILE_FEATS))
    by_half = [
        group * device_list + 2 * pair + side for side in range(2) for group in range(groups) for pair in range(half)
    ]
    partial = lax.all_to_all(
        partial, ("groups", "dp"), split_axis=0, concat_axis=0, axis_index_groups=[by_half], tiled=True
    )
    return jnp.sum(partial, axis=0)


def solution(mesh):
    in_specs = (
        P(("groups", "dp"), None),
        P(("groups", "dp"), None),
        P(("groups", "dp")),
        P("dp", None),
        P("dp", None),
        P(),
    )
    out_specs = P(("groups", "dp"), None)
    return jax.shard_map(local, mesh=mesh, in_specs=in_specs, out_specs=out_specs, check_vma=False)
```

```python
import functools
import math

import jax
import jax.numpy as jnp
from jax import lax
from jax.experimental import pallas as pl
from jax.experimental.pallas import tpu as pltpu
from jax.sharding import PartitionSpec as P

FEAT_BLOCK = 512
beta_one = 0.9
beta_two = 0.999
epsilon = 1e-08
mix_feature = 1640531527
mix_param = 2028178513
mix_round = 73244475
DIGITS = 4
RADIX = 16.0
FP8 = jnp.float8_e4m3fn
STEP_ROWS = 4096
KEPT_ROWS = 1536
TILES = (1280, 1024, 256)
EARLY_ROWS, EARLY_BLOCK = 1536, 512
LATER_BLOCK = 768
TILE_FEATS = 2048


def wrap(value):
    value &= 0xFFFFFFFF
    return jnp.int32(value - (1 << 32) if value >= (1 << 31) else value)


def scramble(hashed):
    hashed = hashed ^ lax.shift_right_logical(hashed, jnp.full_like(hashed, 16))
    hashed = hashed * mix_round
    hashed = hashed ^ lax.shift_right_logical(hashed, jnp.full_like(hashed, 16))
    return hashed * mix_round


def feature_tile(turn):
    core = lax.axis_index("dp") & 1
    return turn ^ (1 - core)


def strides(rows, rank):
    return (1, rank) if rows % 128 == 0 else (rank, 1)


def minor_size(rows, rank):
    return rows if rows % 128 == 0 else rank


def step_start(rows, rank, groups, step):
    mine = lax.axis_index("dp") * groups + lax.axis_index("groups")
    return mine * (rows * rank) + step * (STEP_ROWS // minor_size(rows, rank) * strides(rows, rank)[0])


def hash_base(seed_ref, feature_tile, start, minor_stride):
    pieces = []
    for piece in range(TILE_FEATS // FEAT_BLOCK):
        block = feature_tile * (TILE_FEATS // FEAT_BLOCK) + piece
        down = lax.broadcasted_iota(jnp.int32, (8, FEAT_BLOCK), 0)
        across = lax.broadcasted_iota(jnp.int32, (8, FEAT_BLOCK), 1)
        scalar = seed_ref[block] + block * wrap(FEAT_BLOCK * mix_feature) + start * wrap(mix_param)
        pieces.append(down * wrap(mix_param * minor_stride) + across * wrap(mix_feature) + scalar)
    return jnp.concatenate(pieces, axis=1)


def write_signs(base, rows, rank, offset, count, out_ref):
    minor, (major_stride, minor_stride) = minor_size(rows, rank), strides(rows, rank)
    for top in range(0, count, 32):
        hashes = []
        for part in range(offset + top, offset + top + 32, 8):
            apart = part // minor * major_stride + part % minor * minor_stride
            hashes.append(scramble(base + wrap(mix_param * apart)))
        hashed = jnp.concatenate(hashes, axis=0)
        out_ref[pl.ds(top, 32), :] = jnp.where(hashed < 0, FP8(-1), FP8(1))


def gradient_kernel(away, inputs_ref, cotangent_ref, tokens_ref, *refs):
    *ends, inputs, cotangent, tokens, result, sems, out_sems = refs
    other_ref, out_ref = (None, ends[0]) if away else (ends[0], ends[2])
    groups, pairs, _, rows = out_ref.shape
    width = groups * rows
    side = lax.axis_index("dp") & 1
    side = 1 - side if away else side
    small = [
        pltpu.make_async_copy(cotangent_ref, cotangent, sems.at[pairs]),
        pltpu.make_async_copy(tokens_ref, tokens, sems.at[pairs + 1]),
    ]
    large = []
    for pair in range(pairs):
        columns = pl.ds(pl.multiple_of((2 * pair + side) * width, 128), width)
        large.append(pltpu.make_async_copy(inputs_ref.at[:, columns], inputs.at[pair], sems.at[pair]))
    for copy in small + large:
        copy.start()
    for copy in small:
        copy.wait()
    turned = cotangent[...].astype(jnp.float32).T
    masked = jnp.where(tokens[...] != 0, turned, 0.0).astype(jnp.bfloat16)
    copies = []
    for pair in range(pairs):
        large[pair].wait()
        part = jnp.dot(masked, inputs[pair], preferred_element_type=jnp.float32)
        for group in range(groups):
            piece = part[:, group * rows : (group + 1) * rows]
            if other_ref is not None:
                piece = piece + other_ref[group, pair]
            result[group, pair] = piece
            copies.append(
                pltpu.make_async_copy(
                    result.at[group, pair], out_ref.at[group, pair], out_sems.at[group, pair]
                )
            )
            copies[-1].start()
    for copy in copies:
        copy.wait()


def half_gradient(inputs, cotangent, tokens, away, groups, rows, other=None, after=None):
    count, width = inputs.shape
    rank = cotangent.shape[1]
    pairs = width // (2 * groups * rows)
    if rows % 128:
        side = lax.axis_index("dp") & 1
        side = 1 - side if away else side
        masked = jnp.where((tokens != 0)[:, None], cotangent, jnp.bfloat16(0))
        whole = lax.dot_general(
            inputs, masked, (((0,), (0,)), ((), ())), preferred_element_type=jnp.float32
        )
        whole = whole.reshape(pairs, 2, groups, rows, rank)
        mine = lax.dynamic_index_in_dim(whole, side, 1, keepdims=False).swapaxes(0, 1)
        if away:
            return mine
        other, _ = lax.optimization_barrier((other, after))
        return mine + other
    in_specs = [pl.BlockSpec(memory_space=pltpu.HBM)] * 3
    operands = [inputs, cotangent, tokens[None, :]]
    if not away:
        in_specs += [pl.BlockSpec(memory_space=pltpu.VMEM), pl.BlockSpec(memory_space=pl.ANY)]
        operands += [other, after]
    return pl.pallas_call(
        functools.partial(gradient_kernel, away),
        in_specs=in_specs,
        out_specs=pl.BlockSpec(memory_space=pl.ANY),
        out_shape=jax.ShapeDtypeStruct((groups, pairs, rank, rows), jnp.float32),
        scratch_shapes=[
            pltpu.VMEM((pairs, count, groups * rows), jnp.bfloat16),
            pltpu.VMEM((count, rank), jnp.bfloat16),
            pltpu.VMEM((1, count), jnp.int32),
            pltpu.VMEM((groups, pairs, rank, rows), jnp.float32),
            pltpu.SemaphoreType.DMA((pairs + 2,)),
            pltpu.SemaphoreType.DMA((groups, pairs)),
        ],
        compiler_params=pltpu.CompilerParams(vmem_limit_bytes=None if away else 12 << 20),
        cost_estimate=pl.CostEstimate(
            flops=count * width * rank, bytes_accessed=count * width + 4 * width * rank, transcendentals=0
        ),
        name="half_gradient",
    )(*operands)


def signs_kernel(rows, groups, rank, first, seed_ref, *refs):
    out_ref = refs[-1]
    count = out_ref.shape[0]
    tiles = seed_ref.shape[0] * FEAT_BLOCK // TILE_FEATS
    row = first + pl.program_id(0) // tiles * count
    start = step_start(rows, rank, groups, row // KEPT_ROWS)
    start += row % KEPT_ROWS // minor_size(rows, rank) * strides(rows, rank)[0]
    base = hash_base(seed_ref, feature_tile(pl.program_id(0) % tiles), start, strides(rows, rank)[1])
    write_signs(base, rows, rank, 0, count, out_ref)


def kept_signs(seeds, rows, groups, rank, first, last, block, before=None):
    features = seeds.shape[0] * FEAT_BLOCK
    tiles = features // TILE_FEATS
    size = (last - first) * features
    return pl.pallas_call(
        functools.partial(signs_kernel, rows, groups, rank, first),
        grid=((last - first) // block * tiles,),
        in_specs=[pl.BlockSpec(memory_space=pltpu.SMEM)]
        + [pl.BlockSpec(memory_space=pl.ANY)] * (before is not None),
        out_specs=pl.BlockSpec(
            (block, TILE_FEATS), lambda index: (first // block + index // tiles, index % tiles)
        ),
        out_shape=jax.ShapeDtypeStruct((rows * rank // STEP_ROWS * KEPT_ROWS, features), FP8),
        input_output_aliases={} if before is None else {1: 0},
        compiler_params=pltpu.CompilerParams(vmem_limit_bytes=16 << 20),
        cost_estimate=pl.CostEstimate(flops=size * 10, bytes_accessed=size, transcendentals=0),
        name="kept_signs",
    )(seeds, *([] if before is None else [before]))


def direction_kernel(rows, gradient_ref, first_ref, second_ref, out_ref, scale_ref, held, first, second):
    sequences, major, minor = gradient_ref.shape
    mine = pl.ds(pl.multiple_of(lax.axis_index("groups") * rows, 8), rows)
    turn = major != rows
    first[...] = first_ref[mine, :].T if turn else first_ref[mine, :]
    second[...] = second_ref[mine, :].T if turn else second_ref[mine, :]

    def moments(block, largest):
        at = pl.ds(pl.multiple_of(block * 8, 8), 8)
        gradient = gradient_ref[:, at, :]
        moment_one = beta_one * first[at, :][None] + (1 - beta_one) * gradient
        moment_two = beta_two * second[at, :][None] + (1 - beta_two) * gradient * gradient
        direction = moment_one / (moment_two * lax.rsqrt(moment_two) + epsilon)
        direction = direction.astype(jnp.bfloat16).astype(jnp.float32)
        direction = jnp.swapaxes(direction, 0, 1)
        for row in range(8):
            held[block * 8 + row] = direction[row]
        return jnp.maximum(largest, jnp.max(jnp.abs(direction), axis=0))

    largest = lax.fori_loop(0, major // 8, moments, jnp.zeros((sequences, minor), jnp.float32))
    largest = jnp.broadcast_to(jnp.max(largest, axis=1, keepdims=True), (sequences, minor))
    scale = jnp.ones_like(largest)
    for power in (64, 32, 16, 8, 4, 2, 1):
        room = largest * (2.0**power) < RADIX
        largest = jnp.where(room, largest * (2.0**power), largest)
        scale = jnp.where(room, scale * (2.0**power), scale)
    for power in (2, 1):
        over = largest >= RADIX
        largest = jnp.where(over, largest * (0.5**power), largest)
        scale = jnp.where(over, scale * (0.5**power), scale)
    scale_ref[...] = scale

    def split(row, _):
        rest = held[row] * scale
        digits = []
        for _ in range(DIGITS):
            digit = jnp.round(rest)
            digits.append(digit)
            rest = (rest - digit) * RADIX
        out_ref[:, pl.ds(pl.multiple_of(row * minor, minor), minor)] = jnp.concatenate(digits, axis=0).astype(FP8)
        return 0

    lax.fori_loop(0, major, split, 0, unroll=8)


def scaled_direction(gradient, first, second, rows):
    sequences, major, minor = gradient.shape
    return pl.pallas_call(
        functools.partial(direction_kernel, rows),
        out_shape=(
            jax.ShapeDtypeStruct((DIGITS * sequences, major * minor), FP8),
            jax.ShapeDtypeStruct((sequences, minor), jnp.float32),
        ),
        scratch_shapes=[
            pltpu.VMEM((major, sequences, minor), jnp.float32),
            pltpu.VMEM((major, minor), jnp.float32),
            pltpu.VMEM((major, minor), jnp.float32),
        ],
        compiler_params=pltpu.CompilerParams(vmem_limit_bytes=24 << 20),
        cost_estimate=pl.CostEstimate(
            flops=20 * gradient.size, bytes_accessed=5 * gradient.size, transcendentals=2 * gradient.size
        ),
        name="direction",
    )(gradient, first, second)


def project_kernel(turn, rows, groups, rank, final_scale, seed_ref, direction_ref, scale_ref, kept_ref, out_ref, total, kept, sems, *tiles):
    step, steps = pl.program_id(0), pl.num_programs(0)
    sequences = scale_ref.shape[0]
    start = step_start(rows, rank, groups, step)
    last_rows = TILES[-1]
    columns = pl.ds(turn * TILE_FEATS, TILE_FEATS)

    def fetch(index):
        at = pl.ds(pl.multiple_of(index * KEPT_ROWS, KEPT_ROWS), KEPT_ROWS)
        return pltpu.make_async_copy(kept_ref.at[at, columns], kept.at[index % 2], sems.at[index % 2])

    def multiply(at, signs):
        at = pl.ds(pl.multiple_of(at, 256), signs.shape[0])
        total[...] += jnp.dot(direction_ref[:, at], signs[...], preferred_element_type=jnp.float32)

    @pl.when(step == 0)
    def _():
        fetch(step).start()
        total[...] = jnp.zeros_like(total)
        tiles[-1][...] = jnp.zeros_like(tiles[-1])

    @pl.when(step + 1 < steps)
    def _():
        fetch(step + 1).start()

    here = step * STEP_ROWS
    offset = KEPT_ROWS
    base = hash_base(seed_ref, feature_tile(turn), start, strides(rows, rank)[1])
    for index, count in enumerate(TILES):
        write_signs(base, rows, rank, offset, count, tiles[index])
        if index == 0:
            multiply(jnp.maximum(here - last_rows, 0), tiles[-1])
            fetch(step).wait()
            multiply(here, kept.at[step % 2])
        else:
            multiply(here + offset - TILES[index - 1], tiles[index - 1])
        offset += count

    @pl.when(step == steps - 1)
    def _():
        multiply(here + STEP_ROWS - last_rows, tiles[-1])
        inverse = (1.0 / scale_ref[...])[:, :1]
        value = total[(DIGITS - 1) * sequences :, :]
        for digit in reversed(range(DIGITS - 1)):
            value = total[digit * sequences : (digit + 1) * sequences, :] + value * (1.0 / RADIX)
        value = value * inverse * final_scale
        for sequence in range(sequences):
            out_ref[sequence] = value[sequence : sequence + 1, :]


def project(turn, seeds, direction, scale, kept, rows, groups, rank, final_scale):
    sequences = scale.shape[0]
    params = rows * rank
    return pl.pallas_call(
        functools.partial(project_kernel, turn, rows, groups, rank, final_scale),
        grid=(params // STEP_ROWS,),
        in_specs=[
            pl.BlockSpec(memory_space=pltpu.SMEM),
            pl.BlockSpec(memory_space=pltpu.VMEM),
            pl.BlockSpec(memory_space=pltpu.VMEM),
            pl.BlockSpec(memory_space=pl.ANY),
        ],
        out_specs=pl.BlockSpec((sequences, 1, TILE_FEATS), lambda step: (0, 0, 0)),
        out_shape=jax.ShapeDtypeStruct((sequences, 1, TILE_FEATS), jnp.float32),
        scratch_shapes=[
            pltpu.VMEM((DIGITS * sequences, TILE_FEATS), jnp.float32),
            pltpu.VMEM((2, KEPT_ROWS, TILE_FEATS), FP8),
            pltpu.SemaphoreType.DMA((2,)),
        ]
        + [pltpu.VMEM((count, TILE_FEATS), FP8) for count in TILES],
        compiler_params=pltpu.CompilerParams(vmem_limit_bytes=32 << 20),
        cost_estimate=pl.CostEstimate(
            flops=10 * params * TILE_FEATS, bytes_accessed=params * TILE_FEATS // 3, transcendentals=0
        ),
        name="project",
    )(seeds, direction, scale, kept)


def local(
    hidden_input_rows,
    rank_cotangent,
    token_identifiers,
    adam_first_moment,
    adam_second_moment,
    block_seeds,
):
    groups, device_list = lax.axis_size("groups"), lax.axis_size("dp")
    hidden_width = hidden_input_rows.shape[1]
    rank = rank_cotangent.shape[1]
    rows = adam_first_moment.shape[0] // groups
    half = device_list // 2
    kept_rows = rows * rank // STEP_ROWS * KEPT_ROWS
    early = min(EARLY_ROWS, kept_rows // 3)
    held = (rank_cotangent, token_identifiers)

    given = half_gradient(hidden_input_rows, *held, True, groups, rows)
    pairs = [(source, source ^ 1) for source in range(device_list)]
    other = lax.ppermute(given, "dp", pairs)
    kept = kept_signs(block_seeds, rows, groups, rank, 0, early, EARLY_BLOCK)
    summed = half_gradient(hidden_input_rows, *held, False, groups, rows, other, kept)
    everyone = [
        [group * device_list + 2 * pair + side for group in range(groups) for pair in range(half)]
        for side in range(2)
    ]
    summed = summed.reshape((groups * half,) + summed.shape[2:])
    gradient = lax.all_to_all(
        summed, ("groups", "dp"), split_axis=0, concat_axis=0, axis_index_groups=everyone, tiled=True
    )
    kept = kept_signs(block_seeds, rows, groups, rank, early, kept_rows, LATER_BLOCK, kept)
    direction, scale = scaled_direction(gradient, adam_first_moment, adam_second_moment, rows)
    final_scale = 1.0 / math.sqrt(hidden_width * rank)
    shared = (block_seeds, direction, scale, kept, rows, groups, rank, final_scale)
    theirs = project(0, *shared)
    received = lax.ppermute(theirs, "dp", pairs)
    mine = project(1, *shared)
    partial = lax.all_to_all(
        mine + received, ("groups", "dp"), split_axis=0, concat_axis=0, axis_index_groups=everyone, tiled=True
    )
    return jnp.sum(partial, axis=0)


def solution(mesh):
    in_specs = (
        P(("groups", "dp"), None),
        P(("groups", "dp"), None),
        P(("groups", "dp")),
        P("dp", None),
        P("dp", None),
        P(),
    )
    out_specs = P(("groups", "dp"), None)
    return jax.shard_map(local, mesh=mesh, in_specs=in_specs, out_specs=out_specs, check_vma=False)
```

```python
import functools
import math

import jax
import jax.numpy as jnp
from jax import lax
from jax.experimental import pallas as pl
from jax.experimental.pallas import tpu as pltpu
from jax.sharding import PartitionSpec as P

FEAT_BLOCK = 512
beta_one = 0.9
beta_two = 0.999
epsilon = 1e-08
mix_feature = 1640531527
mix_param = 2028178513
mix_round = 73244475
DIGITS = 4
RADIX = 16.0
FP8 = jnp.float8_e4m3fn
STEP_ROWS = 4096
KEPT_ROWS = 1536
TILES = (1280, 1024, 256)
EARLY_ROWS, EARLY_BLOCK = 1024, 512
LATER_BLOCK = 512
TILE_FEATS = 2048


def wrap(value):
    value &= 0xFFFFFFFF
    return jnp.int32(value - (1 << 32) if value >= (1 << 31) else value)


def scramble(hashed):
    hashed = hashed ^ lax.shift_right_logical(hashed, jnp.full_like(hashed, 16))
    hashed = hashed * mix_round
    hashed = hashed ^ lax.shift_right_logical(hashed, jnp.full_like(hashed, 16))
    return hashed * mix_round


def strides(rows, rank):
    return (1, rank) if rows % 128 == 0 else (rank, 1)


def minor_size(rows, rank):
    return rows if rows % 128 == 0 else rank


def step_start(rows, rank, groups, step):
    mine = lax.axis_index("dp") * groups + lax.axis_index("groups")
    return mine * (rows * rank) + step * (STEP_ROWS // minor_size(rows, rank) * strides(rows, rank)[0])


def hash_base(seed_ref, feature_tile, start, minor_stride):
    pieces = []
    for piece in range(TILE_FEATS // FEAT_BLOCK):
        block = feature_tile * (TILE_FEATS // FEAT_BLOCK) + piece
        down = lax.broadcasted_iota(jnp.int32, (8, FEAT_BLOCK), 0)
        across = lax.broadcasted_iota(jnp.int32, (8, FEAT_BLOCK), 1)
        scalar = seed_ref[block] + block * wrap(FEAT_BLOCK * mix_feature) + start * wrap(mix_param)
        pieces.append(down * wrap(mix_param * minor_stride) + across * wrap(mix_feature) + scalar)
    return jnp.concatenate(pieces, axis=1)


def write_signs(base, rows, rank, offset, count, out_ref):
    minor, (major_stride, minor_stride) = minor_size(rows, rank), strides(rows, rank)
    for top in range(0, count, 32):
        hashes = []
        for part in range(offset + top, offset + top + 32, 8):
            apart = part // minor * major_stride + part % minor * minor_stride
            hashes.append(scramble(base + wrap(mix_param * apart)))
        hashed = jnp.concatenate(hashes, axis=0)
        out_ref[pl.ds(top, 32), :] = jnp.where(hashed < 0, FP8(-1), FP8(1))


def masked_turned(cotangent, tokens):
    return jnp.where(tokens != 0, cotangent.astype(jnp.float32).T, 0.0).astype(jnp.bfloat16)


def put(result, out_ref, sems, group, pair, piece):
    result[group, pair] = piece
    copy = pltpu.make_async_copy(result.at[group, pair], out_ref.at[group, pair], sems.at[group, pair])
    copy.start()
    return copy


def given_kernel(inputs_ref, cotangent_ref, tokens_ref, out_ref, inputs, cotangent, tokens, result, sems, out_sems):
    groups, pairs, _, rows = out_ref.shape
    width = groups * rows
    side = 1 - (lax.axis_index("dp") & 1)
    small = [
        pltpu.make_async_copy(cotangent_ref, cotangent, sems.at[pairs]),
        pltpu.make_async_copy(tokens_ref, tokens, sems.at[pairs + 1]),
    ]
    large = []
    for pair in range(pairs):
        columns = pl.ds(pl.multiple_of((2 * pair + side) * width, 128), width)
        large.append(pltpu.make_async_copy(inputs_ref.at[:, columns], inputs.at[pair], sems.at[pair]))
    for copy in small + large:
        copy.start()
    for copy in small:
        copy.wait()
    masked = masked_turned(cotangent[...], tokens[...])
    copies = []
    for pair in range(pairs):
        large[pair].wait()
        part = jnp.dot(masked, inputs[pair], preferred_element_type=jnp.float32)
        for group in range(groups):
            copies.append(put(result, out_ref, out_sems, group, pair, part[:, group * rows : (group + 1) * rows]))
    for copy in copies:
        copy.wait()


def summed_kernel(inputs_ref, cotangent_ref, tokens_ref, other_ref, after_ref, out_ref, result, out_sems):
    groups, pairs, _, rows = out_ref.shape
    width = groups * rows
    side = lax.axis_index("dp") & 1
    masked = masked_turned(cotangent_ref[...], tokens_ref[...])
    copies = []
    for pair in range(pairs):
        columns = pl.ds(pl.multiple_of((2 * pair + side) * width, 128), width)
        part = jnp.dot(masked, inputs_ref[:, columns], preferred_element_type=jnp.float32)
        for group in range(groups):
            piece = part[:, group * rows : (group + 1) * rows] + other_ref[group, pair]
            copies.append(put(result, out_ref, out_sems, group, pair, piece))
    for copy in copies:
        copy.wait()


def half_gradient(inputs, cotangent, tokens, away, groups, rows, other=None, after=None):
    count, width = inputs.shape
    rank = cotangent.shape[1]
    pairs = width // (2 * groups * rows)
    if rows % 128:
        side = lax.axis_index("dp") & 1
        side = 1 - side if away else side
        masked = jnp.where((tokens != 0)[:, None], cotangent, jnp.bfloat16(0))
        whole = lax.dot_general(
            inputs, masked, (((0,), (0,)), ((), ())), preferred_element_type=jnp.float32
        )
        whole = whole.reshape(pairs, 2, groups, rows, rank)
        mine = lax.dynamic_index_in_dim(whole, side, 1, keepdims=False).swapaxes(0, 1)
        if away:
            return mine
        other, _ = lax.optimization_barrier((other, after))
        return mine + other
    operands = [inputs, cotangent, tokens[None, :]]
    result = pltpu.VMEM((groups, pairs, rank, rows), jnp.float32)
    out_sems = pltpu.SemaphoreType.DMA((groups, pairs))
    if away:
        in_specs = [pl.BlockSpec(memory_space=pl.ANY)] * 3
        scratch = [
            pltpu.VMEM((pairs, count, groups * rows), jnp.bfloat16),
            pltpu.VMEM((count, rank), jnp.bfloat16),
            pltpu.VMEM((1, count), jnp.int32),
            result,
            pltpu.SemaphoreType.DMA((pairs + 2,)),
            out_sems,
        ]
    else:
        in_specs = [pl.BlockSpec(memory_space=pltpu.VMEM)] * 4 + [pl.BlockSpec(memory_space=pl.ANY)]
        operands += [other, after]
        scratch = [result, out_sems]
    return pl.pallas_call(
        given_kernel if away else summed_kernel,
        in_specs=in_specs,
        out_specs=pl.BlockSpec(memory_space=pl.ANY),
        out_shape=jax.ShapeDtypeStruct((groups, pairs, rank, rows), jnp.float32),
        scratch_shapes=scratch,
        compiler_params=pltpu.CompilerParams(vmem_limit_bytes=None if away else 12 << 20),
        cost_estimate=pl.CostEstimate(
            flops=count * width * rank, bytes_accessed=count * width + 4 * width * rank, transcendentals=0
        ),
        name="half_gradient",
    )(*operands)


def signs_kernel(rows, groups, rank, first, seed_ref, *refs):
    out_ref = refs[-1]
    count = out_ref.shape[0]
    tiles = seed_ref.shape[0] * FEAT_BLOCK // TILE_FEATS
    row = first + pl.program_id(0) // tiles * count
    start = step_start(rows, rank, groups, row // KEPT_ROWS)
    start += row % KEPT_ROWS // minor_size(rows, rank) * strides(rows, rank)[0]
    base = hash_base(seed_ref, pl.program_id(0) % tiles, start, strides(rows, rank)[1])
    write_signs(base, rows, rank, 0, count, out_ref)


def kept_signs(seeds, rows, groups, rank, first, last, block, before=None):
    features = seeds.shape[0] * FEAT_BLOCK
    tiles = features // TILE_FEATS
    size = (last - first) * features
    return pl.pallas_call(
        functools.partial(signs_kernel, rows, groups, rank, first),
        grid=((last - first) // block * tiles,),
        in_specs=[pl.BlockSpec(memory_space=pltpu.SMEM)]
        + [pl.BlockSpec(memory_space=pl.ANY)] * (before is not None),
        out_specs=pl.BlockSpec(
            (block, TILE_FEATS), lambda index: (first // block + index // tiles, index % tiles)
        ),
        out_shape=jax.ShapeDtypeStruct((rows * rank // STEP_ROWS * KEPT_ROWS, features), FP8),
        input_output_aliases={} if before is None else {1: 0},
        compiler_params=pltpu.CompilerParams(vmem_limit_bytes=16 << 20),
        cost_estimate=pl.CostEstimate(flops=size * 10, bytes_accessed=size, transcendentals=0),
        name="kept_signs",
    )(seeds, *([] if before is None else [before]))


def direction_kernel(rows, gradient_ref, first_ref, second_ref, out_ref, scale_ref, held, first, second):
    sequences, major, minor = gradient_ref.shape
    mine = pl.ds(pl.multiple_of(lax.axis_index("groups") * rows, 8), rows)
    turn = major != rows
    first[...] = first_ref[mine, :].T if turn else first_ref[mine, :]
    second[...] = second_ref[mine, :].T if turn else second_ref[mine, :]

    def moments(block, largest):
        at = pl.ds(pl.multiple_of(block * 8, 8), 8)
        gradient = gradient_ref[:, at, :]
        moment_one = beta_one * first[at, :][None] + (1 - beta_one) * gradient
        moment_two = beta_two * second[at, :][None] + (1 - beta_two) * gradient * gradient
        direction = moment_one / (moment_two * lax.rsqrt(moment_two) + epsilon)
        direction = direction.astype(jnp.bfloat16).astype(jnp.float32)
        direction = jnp.swapaxes(direction, 0, 1)
        for row in range(8):
            held[block * 8 + row] = direction[row]
        return jnp.maximum(largest, jnp.max(jnp.abs(direction), axis=0))

    largest = lax.fori_loop(0, major // 8, moments, jnp.zeros((sequences, minor), jnp.float32))
    largest = jnp.broadcast_to(jnp.max(largest, axis=1, keepdims=True), (sequences, minor))
    scale = jnp.ones_like(largest)
    for power in (64, 32, 16, 8, 4, 2, 1):
        room = largest * (2.0**power) < RADIX
        largest = jnp.where(room, largest * (2.0**power), largest)
        scale = jnp.where(room, scale * (2.0**power), scale)
    for power in (2, 1):
        over = largest >= RADIX
        largest = jnp.where(over, largest * (0.5**power), largest)
        scale = jnp.where(over, scale * (0.5**power), scale)
    scale_ref[...] = scale

    def split(row, _):
        rest = held[row] * scale
        digits = []
        for _ in range(DIGITS):
            digit = jnp.round(rest)
            digits.append(digit)
            rest = (rest - digit) * RADIX
        out_ref[:, pl.ds(pl.multiple_of(row * minor, minor), minor)] = jnp.concatenate(digits, axis=0).astype(FP8)
        return 0

    lax.fori_loop(0, major, split, 0, unroll=8)


def scaled_direction(gradient, first, second, rows):
    sequences, major, minor = gradient.shape
    return pl.pallas_call(
        functools.partial(direction_kernel, rows),
        out_shape=(
            jax.ShapeDtypeStruct((DIGITS * sequences, major * minor), FP8),
            jax.ShapeDtypeStruct((sequences, minor), jnp.float32),
        ),
        scratch_shapes=[
            pltpu.VMEM((major, sequences, minor), jnp.float32),
            pltpu.VMEM((major, minor), jnp.float32),
            pltpu.VMEM((major, minor), jnp.float32),
        ],
        compiler_params=pltpu.CompilerParams(vmem_limit_bytes=24 << 20),
        cost_estimate=pl.CostEstimate(
            flops=20 * gradient.size, bytes_accessed=5 * gradient.size, transcendentals=2 * gradient.size
        ),
        name="direction",
    )(gradient, first, second)


def project_kernel(rows, groups, rank, final_scale, seed_ref, direction_ref, scale_ref, kept_ref, out_ref, total, *tiles):
    tile, step = pl.program_id(0), pl.program_id(1)
    sequences = scale_ref.shape[0]
    start = step_start(rows, rank, groups, step)
    last_rows = TILES[-1]

    def multiply(at, signs):
        at = pl.ds(pl.multiple_of(at, 256), signs.shape[0])
        total[...] += jnp.dot(direction_ref[:, at], signs[...], preferred_element_type=jnp.float32)

    @pl.when(step == 0)
    def _():
        total[...] = jnp.zeros_like(total)
        tiles[-1][...] = jnp.zeros_like(tiles[-1])

    here = step * STEP_ROWS
    offset = KEPT_ROWS
    base = hash_base(seed_ref, tile, start, strides(rows, rank)[1])
    for index, count in enumerate(TILES):
        write_signs(base, rows, rank, offset, count, tiles[index])
        if index == 0:
            multiply(jnp.maximum(here - last_rows, 0), tiles[-1])
            multiply(here, kept_ref)
        else:
            multiply(here + offset - TILES[index - 1], tiles[index - 1])
        offset += count

    @pl.when(step == pl.num_programs(1) - 1)
    def _():
        multiply(here + STEP_ROWS - last_rows, tiles[-1])
        inverse = (1.0 / scale_ref[...])[:, :1]
        value = total[(DIGITS - 1) * sequences :, :]
        for digit in reversed(range(DIGITS - 1)):
            value = total[digit * sequences : (digit + 1) * sequences, :] + value * (1.0 / RADIX)
        value = value * inverse * final_scale
        for sequence in range(sequences):
            out_ref[sequence, 0] = value[sequence : sequence + 1, :]


def project(seeds, direction, scale, kept, rows, groups, rank, final_scale):
    features = seeds.shape[0] * FEAT_BLOCK
    sequences = scale.shape[0]
    params = rows * rank
    steps = params // STEP_ROWS
    return pl.pallas_call(
        functools.partial(project_kernel, rows, groups, rank, final_scale),
        grid=(features // TILE_FEATS, steps),
        in_specs=[
            pl.BlockSpec(memory_space=pltpu.SMEM),
            pl.BlockSpec((DIGITS * sequences, params), lambda tile, step: (0, 0)),
            pl.BlockSpec(scale.shape, lambda tile, step: (0, 0)),
            pl.BlockSpec((KEPT_ROWS, TILE_FEATS), lambda tile, step: (step, tile)),
        ],
        out_specs=pl.BlockSpec((sequences, 1, 1, TILE_FEATS), lambda tile, step: (0, tile, 0, 0)),
        out_shape=jax.ShapeDtypeStruct((sequences, features // TILE_FEATS, 1, TILE_FEATS), jnp.float32),
        scratch_shapes=[pltpu.VMEM((DIGITS * sequences, TILE_FEATS), jnp.float32)]
        + [pltpu.VMEM((count, TILE_FEATS), FP8) for count in TILES],
        compiler_params=pltpu.CompilerParams(vmem_limit_bytes=32 << 20),
        cost_estimate=pl.CostEstimate(
            flops=10 * params * features, bytes_accessed=params * features // 4, transcendentals=0
        ),
        name="project",
    )(seeds, direction, scale, kept)


def local(
    hidden_input_rows,
    rank_cotangent,
    token_identifiers,
    adam_first_moment,
    adam_second_moment,
    block_seeds,
):
    groups, device_list = lax.axis_size("groups"), lax.axis_size("dp")
    hidden_width = hidden_input_rows.shape[1]
    rank = rank_cotangent.shape[1]
    rows = adam_first_moment.shape[0] // groups
    half = device_list // 2
    kept_rows = rows * rank // STEP_ROWS * KEPT_ROWS
    early = min(EARLY_ROWS, kept_rows // 3)
    held = (rank_cotangent, token_identifiers)

    given = half_gradient(hidden_input_rows, *held, True, groups, rows)
    pairs = [(source, source ^ 1) for source in range(device_list)]
    other = lax.ppermute(given, "dp", pairs)
    kept = kept_signs(block_seeds, rows, groups, rank, 0, early, EARLY_BLOCK)
    summed = half_gradient(hidden_input_rows, *held, False, groups, rows, other, kept)
    everyone = [
        [group * device_list + 2 * pair + side for group in range(groups) for pair in range(half)]
        for side in range(2)
    ]
    summed = summed.reshape((groups * half,) + summed.shape[2:])
    gradient = lax.all_to_all(
        summed, ("groups", "dp"), split_axis=0, concat_axis=0, axis_index_groups=everyone, tiled=True
    )
    kept = kept_signs(block_seeds, rows, groups, rank, early, kept_rows, LATER_BLOCK, kept)
    direction, scale = scaled_direction(gradient, adam_first_moment, adam_second_moment, rows)
    final_scale = 1.0 / math.sqrt(hidden_width * rank)
    partial = project(block_seeds, direction, scale, kept, rows, groups, rank, final_scale)
    partial = partial.reshape((groups * device_list, 1, TILE_FEATS))
    partial = lax.all_to_all(partial, ("groups", "dp"), split_axis=0, concat_axis=0, tiled=True)
    return jnp.sum(partial, axis=0)


def solution(mesh):
    in_specs = (
        P(("groups", "dp"), None),
        P(("groups", "dp"), None),
        P(("groups", "dp")),
        P("dp", None),
        P("dp", None),
        P(),
    )
    out_specs = P(("groups", "dp"), None)
    return jax.shard_map(local, mesh=mesh, in_specs=in_specs, out_specs=out_specs, check_vma=False)
```

```python
import functools
import math

import jax
import jax.numpy as jnp
from jax import lax
from jax.experimental import pallas as pl
from jax.experimental.pallas import tpu as pltpu
from jax.sharding import PartitionSpec as P

FEAT_BLOCK = 512
beta_one = 0.9
beta_two = 0.999
epsilon = 1e-08
mix_feature = 1640531527
mix_param = 2028178513
mix_round = 73244475
DIGITS = 4
RADIX = 16.0
FP8 = jnp.float8_e4m3fn
STEP_ROWS = 4096
KEPT_ROWS = 1536
TILES = (1280, 1024, 256)
EARLY_ROWS, EARLY_BLOCK = 768, 384
LATER_BLOCK = 768
LANES = 128
TILE_FEATS = 2048


def wrap(value):
    value &= 0xFFFFFFFF
    return jnp.int32(value - (1 << 32) if value >= (1 << 31) else value)


def scramble(hashed):
    hashed = hashed ^ lax.shift_right_logical(hashed, jnp.full_like(hashed, 16))
    hashed = hashed * mix_round
    hashed = hashed ^ lax.shift_right_logical(hashed, jnp.full_like(hashed, 16))
    return hashed * mix_round


def turned(rows):
    return rows % LANES == 0


def strides(rows, rank):
    return (1, rank) if turned(rows) else (rank, 1)


def step_start(rows, rank, groups, step):
    mine = lax.axis_index("dp") * groups + lax.axis_index("groups")
    line = step * (STEP_ROWS // LANES)
    apart = line // rank * (LANES * rank) + line % rank if turned(rows) else line * rank
    return mine * (rows * rank) + apart


def hash_base(seed_ref, feature_tile, start, minor_stride):
    pieces = []
    for piece in range(TILE_FEATS // FEAT_BLOCK):
        block = feature_tile * (TILE_FEATS // FEAT_BLOCK) + piece
        down = lax.broadcasted_iota(jnp.int32, (8, FEAT_BLOCK), 0)
        across = lax.broadcasted_iota(jnp.int32, (8, FEAT_BLOCK), 1)
        scalar = seed_ref[block] + block * wrap(FEAT_BLOCK * mix_feature) + start * wrap(mix_param)
        pieces.append(down * wrap(mix_param * minor_stride) + across * wrap(mix_feature) + scalar)
    return jnp.concatenate(pieces, axis=1)


def write_signs(base, rows, rank, offset, count, out_ref):
    major_stride, minor_stride = strides(rows, rank)
    for top in range(0, count, 32):
        hashes = []
        for part in range(offset + top, offset + top + 32, 8):
            apart = part // LANES * major_stride + part % LANES * minor_stride
            hashes.append(scramble(base + wrap(mix_param * apart)))
        hashed = jnp.concatenate(hashes, axis=0)
        out_ref[pl.ds(top, 32), :] = jnp.where(hashed < 0, FP8(-1), FP8(1))


def masked_turned(cotangent, tokens):
    return jnp.where(tokens != 0, cotangent.astype(jnp.float32).T, 0.0).astype(jnp.bfloat16)


def put(result, out_ref, sems, group, pair, part, other_ref=None):
    rank = part.shape[0]
    lines = result.shape[2] // rank
    for line in range(lines):
        left = (group * lines + line) * LANES
        at = slice(line * rank, (line + 1) * rank)
        piece = part[:, left : left + LANES]
        result[group, pair, at, :] = piece if other_ref is None else piece + other_ref[group, pair, at, :]
    copy = pltpu.make_async_copy(result.at[group, pair], out_ref.at[group, pair], sems.at[group, pair])
    copy.start()
    return copy


def given_kernel(inputs_ref, cotangent_ref, tokens_ref, out_ref, inputs, cotangent, tokens, result, sems, out_sems):
    groups, pairs = out_ref.shape[:2]
    width = inputs.shape[2]
    side = 1 - (lax.axis_index("dp") & 1)
    small = [
        pltpu.make_async_copy(cotangent_ref, cotangent, sems.at[pairs]),
        pltpu.make_async_copy(tokens_ref, tokens, sems.at[pairs + 1]),
    ]
    large = []
    for pair in range(pairs):
        columns = pl.ds(pl.multiple_of((2 * pair + side) * width, 128), width)
        large.append(pltpu.make_async_copy(inputs_ref.at[:, columns], inputs.at[pair], sems.at[pair]))
    for copy in small + large:
        copy.start()
    for copy in small:
        copy.wait()
    masked = masked_turned(cotangent[...], tokens[...])
    copies = []
    for pair in range(pairs):
        large[pair].wait()
        part = jnp.dot(masked, inputs[pair], preferred_element_type=jnp.float32)
        for group in range(groups):
            copies.append(put(result, out_ref, out_sems, group, pair, part))
    for copy in copies:
        copy.wait()


def summed_kernel(inputs_ref, cotangent_ref, tokens_ref, other_ref, after_ref, out_ref, result, out_sems):
    groups, pairs = out_ref.shape[:2]
    width = inputs_ref.shape[1] // (2 * pairs)
    side = lax.axis_index("dp") & 1
    masked = masked_turned(cotangent_ref[...], tokens_ref[...])
    copies = []
    for pair in range(pairs):
        columns = pl.ds(pl.multiple_of((2 * pair + side) * width, 128), width)
        part = jnp.dot(masked, inputs_ref[:, columns], preferred_element_type=jnp.float32)
        for group in range(groups):
            copies.append(put(result, out_ref, out_sems, group, pair, part, other_ref))
    for copy in copies:
        copy.wait()


def half_gradient(inputs, cotangent, tokens, away, groups, rows, other=None, after=None):
    count, width = inputs.shape
    rank = cotangent.shape[1]
    pairs = width // (2 * groups * rows)
    if not turned(rows):
        side = lax.axis_index("dp") & 1
        side = 1 - side if away else side
        masked = jnp.where((tokens != 0)[:, None], cotangent, jnp.bfloat16(0))
        whole = lax.dot_general(
            inputs, masked, (((0,), (0,)), ((), ())), preferred_element_type=jnp.float32
        )
        whole = whole.reshape(pairs, 2, groups, rows, rank)
        mine = lax.dynamic_index_in_dim(whole, side, 1, keepdims=False).swapaxes(0, 1)
        if away:
            return mine
        other, _ = lax.optimization_barrier((other, after))
        return mine + other
    operands = [inputs, cotangent, tokens[None, :]]
    result = pltpu.VMEM((groups, pairs, rows // LANES * rank, LANES), jnp.float32)
    out_sems = pltpu.SemaphoreType.DMA((groups, pairs))
    if away:
        in_specs = [pl.BlockSpec(memory_space=pl.ANY)] * 3
        scratch = [
            pltpu.VMEM((pairs, count, groups * rows), jnp.bfloat16),
            pltpu.VMEM((count, rank), jnp.bfloat16),
            pltpu.VMEM((1, count), jnp.int32),
            result,
            pltpu.SemaphoreType.DMA((pairs + 2,)),
            out_sems,
        ]
    else:
        in_specs = [pl.BlockSpec(memory_space=pltpu.VMEM)] * 4 + [pl.BlockSpec(memory_space=pl.ANY)]
        operands += [other, after]
        scratch = [result, out_sems]
    return pl.pallas_call(
        given_kernel if away else summed_kernel,
        in_specs=in_specs,
        out_specs=pl.BlockSpec(memory_space=pl.ANY),
        out_shape=jax.ShapeDtypeStruct((groups, pairs, rows // LANES * rank, LANES), jnp.float32),
        scratch_shapes=scratch,
        compiler_params=pltpu.CompilerParams(vmem_limit_bytes=None if away else 12 << 20),
        cost_estimate=pl.CostEstimate(
            flops=count * width * rank, bytes_accessed=count * width + 4 * width * rank, transcendentals=0
        ),
        name="half_gradient",
    )(*operands)


def signs_kernel(rows, groups, rank, first, seed_ref, *refs):
    out_ref = refs[-1]
    count = out_ref.shape[0]
    tiles = seed_ref.shape[0] * FEAT_BLOCK // TILE_FEATS
    row = first + pl.program_id(0) // tiles * count
    start = step_start(rows, rank, groups, row // KEPT_ROWS)
    start += row % KEPT_ROWS // LANES * strides(rows, rank)[0]
    base = hash_base(seed_ref, pl.program_id(0) % tiles, start, strides(rows, rank)[1])
    write_signs(base, rows, rank, 0, count, out_ref)


def kept_signs(seeds, rows, groups, rank, first, last, block, before=None):
    features = seeds.shape[0] * FEAT_BLOCK
    tiles = features // TILE_FEATS
    size = (last - first) * features
    return pl.pallas_call(
        functools.partial(signs_kernel, rows, groups, rank, first),
        grid=((last - first) // block * tiles,),
        in_specs=[pl.BlockSpec(memory_space=pltpu.SMEM)]
        + [pl.BlockSpec(memory_space=pl.ANY)] * (before is not None),
        out_specs=pl.BlockSpec(
            (block, TILE_FEATS), lambda index: (first // block + index // tiles, index % tiles)
        ),
        out_shape=jax.ShapeDtypeStruct((rows * rank // STEP_ROWS * KEPT_ROWS, features), FP8),
        input_output_aliases={} if before is None else {1: 0},
        compiler_params=pltpu.CompilerParams(vmem_limit_bytes=16 << 20),
        cost_estimate=pl.CostEstimate(flops=size * 10, bytes_accessed=size, transcendentals=0),
        name="kept_signs",
    )(seeds, *([] if before is None else [before]))


def direction_kernel(rows, gradient_ref, first_ref, second_ref, out_ref, scale_ref, held, first, second):
    major, sequences, minor = held.shape
    mine = pl.ds(pl.multiple_of(lax.axis_index("groups") * rows, 8), rows)
    for moment, moment_ref, beta in ((first, first_ref, beta_one), (second, second_ref, beta_two)):
        values = beta * moment_ref[mine, :]
        rank = values.shape[1]
        if not turned(rows):
            moment[...] = values
            continue
        for line in range(rows // LANES):
            moment[line * rank : (line + 1) * rank, :] = values[line * LANES : (line + 1) * LANES, :].T

    def moments(row, largest):
        gradient = gradient_ref[pl.ds(row, sequences, stride=major), :]
        moment_one = first[pl.ds(row, 1), :] + (1 - beta_one) * gradient
        moment_two = second[pl.ds(row, 1), :] + (1 - beta_two) * gradient * gradient
        direction = moment_one / (moment_two * lax.rsqrt(moment_two) + epsilon)
        direction = direction.astype(jnp.bfloat16).astype(jnp.float32)
        held[row] = direction
        return jnp.maximum(largest, jnp.abs(direction))

    largest = lax.fori_loop(0, major, moments, jnp.zeros((sequences, minor), jnp.float32), unroll=8)
    largest = jnp.broadcast_to(jnp.max(largest, axis=1, keepdims=True), (sequences, minor))
    scale = jnp.ones_like(largest)
    for power in (64, 32, 16, 8, 4, 2, 1):
        room = largest * (2.0**power) < RADIX
        largest = jnp.where(room, largest * (2.0**power), largest)
        scale = jnp.where(room, scale * (2.0**power), scale)
    for power in (2, 1):
        over = largest >= RADIX
        largest = jnp.where(over, largest * (0.5**power), largest)
        scale = jnp.where(over, scale * (0.5**power), scale)
    scale_ref[...] = scale

    def split(row, _):
        rest = held[row] * scale
        digits = []
        for _ in range(DIGITS):
            digit = jnp.round(rest)
            digits.append(digit)
            rest = (rest - digit) * RADIX
        out_ref[:, pl.ds(pl.multiple_of(row * minor, minor), minor)] = jnp.concatenate(digits, axis=0).astype(FP8)
        return 0

    lax.fori_loop(0, major, split, 0, unroll=8)


def scaled_direction(gradient, first, second, rows):
    sequences, major, minor = gradient.shape
    return pl.pallas_call(
        functools.partial(direction_kernel, rows),
        out_shape=(
            jax.ShapeDtypeStruct((DIGITS * sequences, major * minor), FP8),
            jax.ShapeDtypeStruct((sequences, minor), jnp.float32),
        ),
        scratch_shapes=[
            pltpu.VMEM((major, sequences, minor), jnp.float32),
            pltpu.VMEM((major, minor), jnp.float32),
            pltpu.VMEM((major, minor), jnp.float32),
        ],
        compiler_params=pltpu.CompilerParams(vmem_limit_bytes=24 << 20),
        cost_estimate=pl.CostEstimate(
            flops=20 * gradient.size, bytes_accessed=5 * gradient.size, transcendentals=2 * gradient.size
        ),
        name="direction",
    )(gradient.reshape(sequences * major, minor), first, second)


def project_kernel(rows, groups, rank, final_scale, seed_ref, direction_ref, scale_ref, kept_ref, out_ref, total, *tiles):
    tile, step = pl.program_id(0), pl.program_id(1)
    sequences = scale_ref.shape[0]
    start = step_start(rows, rank, groups, step)
    last_rows = TILES[-1]

    def multiply(at, signs):
        at = pl.ds(pl.multiple_of(at, 256), signs.shape[0])
        total[...] += jnp.dot(direction_ref[:, at], signs[...], preferred_element_type=jnp.float32)

    @pl.when(step == 0)
    def _():
        total[...] = jnp.zeros_like(total)
        tiles[-1][...] = jnp.zeros_like(tiles[-1])

    here = step * STEP_ROWS
    offset = KEPT_ROWS
    base = hash_base(seed_ref, tile, start, strides(rows, rank)[1])
    for index, count in enumerate(TILES):
        write_signs(base, rows, rank, offset, count, tiles[index])
        if index == 0:
            multiply(jnp.maximum(here - last_rows, 0), tiles[-1])
            multiply(here, kept_ref)
        else:
            multiply(here + offset - TILES[index - 1], tiles[index - 1])
        offset += count

    @pl.when(step == pl.num_programs(1) - 1)
    def _():
        multiply(here + STEP_ROWS - last_rows, tiles[-1])
        inverse = (1.0 / scale_ref[...])[:, :1]
        value = total[(DIGITS - 1) * sequences :, :]
        for digit in reversed(range(DIGITS - 1)):
            value = total[digit * sequences : (digit + 1) * sequences, :] + value * (1.0 / RADIX)
        value = value * inverse * final_scale
        for sequence in range(sequences):
            out_ref[sequence, 0] = value[sequence : sequence + 1, :]


def project(seeds, direction, scale, kept, rows, groups, rank, final_scale):
    features = seeds.shape[0] * FEAT_BLOCK
    sequences = scale.shape[0]
    params = rows * rank
    steps = params // STEP_ROWS
    return pl.pallas_call(
        functools.partial(project_kernel, rows, groups, rank, final_scale),
        grid=(features // TILE_FEATS, steps),
        in_specs=[
            pl.BlockSpec(memory_space=pltpu.SMEM),
            pl.BlockSpec(memory_space=pltpu.VMEM),
            pl.BlockSpec(memory_space=pltpu.VMEM),
            pl.BlockSpec((KEPT_ROWS, TILE_FEATS), lambda tile, step: (step, tile)),
        ],
        out_specs=pl.BlockSpec((sequences, 1, 1, TILE_FEATS), lambda tile, step: (0, tile, 0, 0)),
        out_shape=jax.ShapeDtypeStruct((sequences, features // TILE_FEATS, 1, TILE_FEATS), jnp.float32),
        scratch_shapes=[pltpu.VMEM((DIGITS * sequences, TILE_FEATS), jnp.float32)]
        + [pltpu.VMEM((count, TILE_FEATS), FP8) for count in TILES],
        compiler_params=pltpu.CompilerParams(vmem_limit_bytes=32 << 20),
        cost_estimate=pl.CostEstimate(
            flops=10 * params * features, bytes_accessed=params * features // 4, transcendentals=0
        ),
        name="project",
    )(seeds, direction, scale, kept)


def local(
    hidden_input_rows,
    rank_cotangent,
    token_identifiers,
    adam_first_moment,
    adam_second_moment,
    block_seeds,
):
    groups, device_list = lax.axis_size("groups"), lax.axis_size("dp")
    hidden_width = hidden_input_rows.shape[1]
    rank = rank_cotangent.shape[1]
    rows = adam_first_moment.shape[0] // groups
    half = device_list // 2
    kept_rows = rows * rank // STEP_ROWS * KEPT_ROWS
    early = min(EARLY_ROWS, kept_rows // 2)
    held = (rank_cotangent, token_identifiers)

    given = half_gradient(hidden_input_rows, *held, True, groups, rows)
    pairs = [(source, source ^ 1) for source in range(device_list)]
    other = lax.ppermute(given, "dp", pairs)
    kept = kept_signs(block_seeds, rows, groups, rank, 0, early, EARLY_BLOCK)
    summed = half_gradient(hidden_input_rows, *held, False, groups, rows, other, kept)
    everyone = [
        [group * device_list + 2 * pair + side for group in range(groups) for pair in range(half)]
        for side in range(2)
    ]
    summed = summed.reshape((groups * half,) + summed.shape[2:])
    gradient = lax.all_to_all(
        summed, ("groups", "dp"), split_axis=0, concat_axis=0, axis_index_groups=everyone, tiled=True
    )
    kept = kept_signs(block_seeds, rows, groups, rank, early, kept_rows, LATER_BLOCK, kept)
    direction, scale = scaled_direction(gradient, adam_first_moment, adam_second_moment, rows)
    final_scale = 1.0 / math.sqrt(hidden_width * rank)
    partial = project(block_seeds, direction, scale, kept, rows, groups, rank, final_scale)
    partial = partial.reshape((groups * device_list, 1, TILE_FEATS))
    partial = lax.all_to_all(partial, ("groups", "dp"), split_axis=0, concat_axis=0, tiled=True)
    return jnp.sum(partial, axis=0)


def solution(mesh):
    in_specs = (
        P(("groups", "dp"), None),
        P(("groups", "dp"), None),
        P(("groups", "dp")),
        P("dp", None),
        P("dp", None),
        P(),
    )
    out_specs = P(("groups", "dp"), None)
    return jax.shard_map(local, mesh=mesh, in_specs=in_specs, out_specs=out_specs, check_vma=False)
```

```python
import functools
import math

import jax
import jax.numpy as jnp
from jax import lax
from jax.experimental import pallas as pl
from jax.experimental.pallas import tpu as pltpu
from jax.sharding import PartitionSpec as P

FEAT_BLOCK = 512
beta_one = 0.9
beta_two = 0.999
epsilon = 1e-08
mix_feature = 1640531527
mix_param = 2028178513
mix_round = 73244475
DIGITS = 4
RADIX = 16.0
FP8 = jnp.float8_e4m3fn
STEP_ROWS = 4096
KEPT_ROWS = 1536
TILES = (1280, 1024, 256)
EARLY_ROWS, EARLY_BLOCK = 1024, 512
LATER_BLOCK = 512
TILE_FEATS = 2048


def wrap(value):
    value &= 0xFFFFFFFF
    return jnp.int32(value - (1 << 32) if value >= (1 << 31) else value)


def scramble(hashed):
    hashed = hashed ^ lax.shift_right_logical(hashed, jnp.full_like(hashed, 16))
    hashed = hashed * mix_round
    hashed = hashed ^ lax.shift_right_logical(hashed, jnp.full_like(hashed, 16))
    return hashed * mix_round


def strides(rows, rank):
    return (1, rank) if rows % 128 == 0 else (rank, 1)


def minor_size(rows, rank):
    return rows if rows % 128 == 0 else rank


def step_start(rows, rank, groups, step):
    mine = lax.axis_index("dp") * groups + lax.axis_index("groups")
    return mine * (rows * rank) + step * (STEP_ROWS // minor_size(rows, rank) * strides(rows, rank)[0])


def hash_base(seed_ref, feature_tile, start, minor_stride):
    pieces = []
    for piece in range(TILE_FEATS // FEAT_BLOCK):
        block = feature_tile * (TILE_FEATS // FEAT_BLOCK) + piece
        down = lax.broadcasted_iota(jnp.int32, (8, FEAT_BLOCK), 0)
        across = lax.broadcasted_iota(jnp.int32, (8, FEAT_BLOCK), 1)
        scalar = seed_ref[block] + block * wrap(FEAT_BLOCK * mix_feature) + start * wrap(mix_param)
        pieces.append(down * wrap(mix_param * minor_stride) + across * wrap(mix_feature) + scalar)
    return jnp.concatenate(pieces, axis=1)


def write_signs(base, rows, rank, offset, count, out_ref):
    minor, (major_stride, minor_stride) = minor_size(rows, rank), strides(rows, rank)
    for top in range(0, count, 32):
        hashes = []
        for part in range(offset + top, offset + top + 32, 8):
            apart = part // minor * major_stride + part % minor * minor_stride
            hashes.append(scramble(base + wrap(mix_param * apart)))
        hashed = jnp.concatenate(hashes, axis=0)
        out_ref[pl.ds(top, 32), :] = jnp.where(hashed < 0, FP8(-1), FP8(1))


def masked_turned(cotangent, tokens):
    return jnp.where(tokens != 0, cotangent.astype(jnp.float32).T, 0.0).astype(jnp.bfloat16)


def put(result, out_ref, sems, group, pair, piece):
    result[group, pair] = piece
    copy = pltpu.make_async_copy(result.at[group, pair], out_ref.at[group, pair], sems.at[group, pair])
    copy.start()
    return copy


def given_kernel(inputs_ref, cotangent_ref, tokens_ref, out_ref, inputs, cotangent, tokens, result, sems, out_sems):
    groups, pairs, _, rows = out_ref.shape
    width = groups * rows
    side = 1 - (lax.axis_index("dp") & 1)
    small = [
        pltpu.make_async_copy(cotangent_ref, cotangent, sems.at[pairs]),
        pltpu.make_async_copy(tokens_ref, tokens, sems.at[pairs + 1]),
    ]
    large = []
    for pair in range(pairs):
        columns = pl.ds(pl.multiple_of((2 * pair + side) * width, 128), width)
        large.append(pltpu.make_async_copy(inputs_ref.at[:, columns], inputs.at[pair], sems.at[pair]))
    for copy in small + large:
        copy.start()
    for copy in small:
        copy.wait()
    masked = masked_turned(cotangent[...], tokens[...])
    copies = []
    for pair in range(pairs):
        large[pair].wait()
        part = jnp.dot(masked, inputs[pair], preferred_element_type=jnp.float32)
        for group in range(groups):
            copies.append(put(result, out_ref, out_sems, group, pair, part[:, group * rows : (group + 1) * rows]))
    for copy in copies:
        copy.wait()


def summed_kernel(inputs_ref, cotangent_ref, tokens_ref, other_ref, after_ref, out_ref, result, out_sems):
    groups, pairs, _, rows = out_ref.shape
    width = groups * rows
    side = lax.axis_index("dp") & 1
    masked = masked_turned(cotangent_ref[...], tokens_ref[...])
    copies = []
    for pair in range(pairs):
        columns = pl.ds(pl.multiple_of((2 * pair + side) * width, 128), width)
        part = jnp.dot(masked, inputs_ref[:, columns], preferred_element_type=jnp.float32)
        for group in range(groups):
            piece = part[:, group * rows : (group + 1) * rows] + other_ref[group, pair]
            copies.append(put(result, out_ref, out_sems, group, pair, piece))
    for copy in copies:
        copy.wait()


def half_gradient(inputs, cotangent, tokens, away, groups, rows, other=None, after=None):
    count, width = inputs.shape
    rank = cotangent.shape[1]
    pairs = width // (2 * groups * rows)
    if rows % 128:
        side = lax.axis_index("dp") & 1
        side = 1 - side if away else side
        masked = jnp.where((tokens != 0)[:, None], cotangent, jnp.bfloat16(0))
        whole = lax.dot_general(
            inputs, masked, (((0,), (0,)), ((), ())), preferred_element_type=jnp.float32
        )
        whole = whole.reshape(pairs, 2, groups, rows, rank)
        mine = lax.dynamic_index_in_dim(whole, side, 1, keepdims=False).swapaxes(0, 1)
        if away:
            return mine
        other, _ = lax.optimization_barrier((other, after))
        return mine + other
    operands = [inputs, cotangent, tokens[None, :]]
    result = pltpu.VMEM((groups, pairs, rank, rows), jnp.float32)
    out_sems = pltpu.SemaphoreType.DMA((groups, pairs))
    if away:
        in_specs = [pl.BlockSpec(memory_space=pl.ANY)] * 3
        scratch = [
            pltpu.VMEM((pairs, count, groups * rows), jnp.bfloat16),
            pltpu.VMEM((count, rank), jnp.bfloat16),
            pltpu.VMEM((1, count), jnp.int32),
            result,
            pltpu.SemaphoreType.DMA((pairs + 2,)),
            out_sems,
        ]
    else:
        in_specs = [pl.BlockSpec(memory_space=pltpu.VMEM)] * 4 + [pl.BlockSpec(memory_space=pl.ANY)]
        operands += [other, after]
        scratch = [result, out_sems]
    return pl.pallas_call(
        given_kernel if away else summed_kernel,
        in_specs=in_specs,
        out_specs=pl.BlockSpec(memory_space=pl.ANY),
        out_shape=jax.ShapeDtypeStruct((groups, pairs, rank, rows), jnp.float32),
        scratch_shapes=scratch,
        compiler_params=pltpu.CompilerParams(vmem_limit_bytes=None if away else 12 << 20),
        cost_estimate=pl.CostEstimate(
            flops=count * width * rank, bytes_accessed=count * width + 4 * width * rank, transcendentals=0
        ),
        name="half_gradient",
    )(*operands)


def signs_kernel(rows, groups, rank, first, seed_ref, *refs):
    out_ref = refs[-1]
    count = out_ref.shape[0]
    tiles = seed_ref.shape[0] * FEAT_BLOCK // TILE_FEATS
    row = first + pl.program_id(0) // tiles * count
    start = step_start(rows, rank, groups, row // KEPT_ROWS)
    start += row % KEPT_ROWS // minor_size(rows, rank) * strides(rows, rank)[0]
    base = hash_base(seed_ref, pl.program_id(0) % tiles, start, strides(rows, rank)[1])
    write_signs(base, rows, rank, 0, count, out_ref)


def kept_signs(seeds, rows, groups, rank, first, last, block, before=None):
    features = seeds.shape[0] * FEAT_BLOCK
    tiles = features // TILE_FEATS
    size = (last - first) * features
    return pl.pallas_call(
        functools.partial(signs_kernel, rows, groups, rank, first),
        grid=((last - first) // block * tiles,),
        in_specs=[pl.BlockSpec(memory_space=pltpu.SMEM)]
        + [pl.BlockSpec(memory_space=pl.ANY)] * (before is not None),
        out_specs=pl.BlockSpec(
            (block, TILE_FEATS), lambda index: (first // block + index // tiles, index % tiles)
        ),
        out_shape=jax.ShapeDtypeStruct((rows * rank // STEP_ROWS * KEPT_ROWS, features), FP8),
        input_output_aliases={} if before is None else {1: 0},
        compiler_params=pltpu.CompilerParams(vmem_limit_bytes=16 << 20),
        cost_estimate=pl.CostEstimate(flops=size * 10, bytes_accessed=size, transcendentals=0),
        name="kept_signs",
    )(seeds, *([] if before is None else [before]))


def direction_kernel(rows, gradient_ref, first_ref, second_ref, out_ref, scale_ref, held, first, second):
    sequences, major, minor = gradient_ref.shape
    mine = pl.ds(pl.multiple_of(lax.axis_index("groups") * rows, 8), rows)
    turn = major != rows
    first[...] = first_ref[mine, :].T if turn else first_ref[mine, :]
    second[...] = second_ref[mine, :].T if turn else second_ref[mine, :]

    def moments(block, largest):
        at = pl.ds(pl.multiple_of(block * 8, 8), 8)
        gradient = gradient_ref[:, at, :]
        moment_one = beta_one * first[at, :][None] + (1 - beta_one) * gradient
        moment_two = beta_two * second[at, :][None] + (1 - beta_two) * gradient * gradient
        direction = moment_one / (moment_two * lax.rsqrt(moment_two) + epsilon)
        direction = direction.astype(jnp.bfloat16).astype(jnp.float32)
        direction = jnp.swapaxes(direction, 0, 1)
        for row in range(8):
            held[block * 8 + row] = direction[row].astype(jnp.bfloat16)
        return jnp.maximum(largest, jnp.max(jnp.abs(direction), axis=0))

    largest = lax.fori_loop(0, major // 8, moments, jnp.zeros((sequences, minor), jnp.float32), unroll=4)
    largest = jnp.broadcast_to(jnp.max(largest, axis=1, keepdims=True), (sequences, minor))
    scale = jnp.ones_like(largest)
    for power in (64, 32, 16, 8, 4, 2, 1):
        room = largest * (2.0**power) < RADIX
        largest = jnp.where(room, largest * (2.0**power), largest)
        scale = jnp.where(room, scale * (2.0**power), scale)
    for power in (2, 1):
        over = largest >= RADIX
        largest = jnp.where(over, largest * (0.5**power), largest)
        scale = jnp.where(over, scale * (0.5**power), scale)
    scale_ref[...] = scale

    narrow = scale.astype(jnp.bfloat16)
    radix, shift = jnp.bfloat16(RADIX), jnp.bfloat16(192.0)

    def split(row, _):
        rest = held[row] * narrow
        digits = []
        for _ in range(DIGITS):
            digit = (rest + shift) - shift
            digits.append(digit)
            rest = (rest - digit) * radix
        out_ref[:, pl.ds(pl.multiple_of(row * minor, minor), minor)] = jnp.concatenate(digits, axis=0).astype(FP8)
        return 0

    lax.fori_loop(0, major, split, 0, unroll=64)


def scaled_direction(gradient, first, second, rows):
    sequences, major, minor = gradient.shape
    return pl.pallas_call(
        functools.partial(direction_kernel, rows),
        out_shape=(
            jax.ShapeDtypeStruct((DIGITS * sequences, major * minor), FP8),
            jax.ShapeDtypeStruct((sequences, minor), jnp.float32),
        ),
        scratch_shapes=[
            pltpu.VMEM((major, sequences, minor), jnp.bfloat16),
            pltpu.VMEM((major, minor), jnp.float32),
            pltpu.VMEM((major, minor), jnp.float32),
        ],
        compiler_params=pltpu.CompilerParams(vmem_limit_bytes=24 << 20),
        cost_estimate=pl.CostEstimate(
            flops=20 * gradient.size, bytes_accessed=5 * gradient.size, transcendentals=2 * gradient.size
        ),
        name="direction",
    )(gradient, first, second)


def project_kernel(rows, groups, rank, final_scale, seed_ref, direction_ref, scale_ref, kept_ref, out_ref, total, *tiles):
    tile, step = pl.program_id(0), pl.program_id(1)
    sequences = scale_ref.shape[0]
    start = step_start(rows, rank, groups, step)
    last_rows = TILES[-1]

    def multiply(at, signs):
        at = pl.ds(pl.multiple_of(at, 256), signs.shape[0])
        total[...] += jnp.dot(direction_ref[:, at], signs[...], preferred_element_type=jnp.float32)

    @pl.when(step == 0)
    def _():
        total[...] = jnp.zeros_like(total)
        tiles[-1][...] = jnp.zeros_like(tiles[-1])

    here = step * STEP_ROWS
    offset = KEPT_ROWS
    base = hash_base(seed_ref, tile, start, strides(rows, rank)[1])
    for index, count in enumerate(TILES):
        write_signs(base, rows, rank, offset, count, tiles[index])
        if index == 0:
            multiply(jnp.maximum(here - last_rows, 0), tiles[-1])
            multiply(here, kept_ref)
        else:
            multiply(here + offset - TILES[index - 1], tiles[index - 1])
        offset += count

    @pl.when(step == pl.num_programs(1) - 1)
    def _():
        multiply(here + STEP_ROWS - last_rows, tiles[-1])
        inverse = (1.0 / scale_ref[...])[:, :1]
        value = total[(DIGITS - 1) * sequences :, :]
        for digit in reversed(range(DIGITS - 1)):
            value = total[digit * sequences : (digit + 1) * sequences, :] + value * (1.0 / RADIX)
        value = value * inverse * final_scale
        for sequence in range(sequences):
            out_ref[sequence, 0] = value[sequence : sequence + 1, :]


def project(seeds, direction, scale, kept, rows, groups, rank, final_scale):
    features = seeds.shape[0] * FEAT_BLOCK
    sequences = scale.shape[0]
    params = rows * rank
    steps = params // STEP_ROWS
    return pl.pallas_call(
        functools.partial(project_kernel, rows, groups, rank, final_scale),
        grid=(features // TILE_FEATS, steps),
        in_specs=[
            pl.BlockSpec(memory_space=pltpu.SMEM),
            pl.BlockSpec((DIGITS * sequences, params), lambda tile, step: (0, 0)),
            pl.BlockSpec(scale.shape, lambda tile, step: (0, 0)),
            pl.BlockSpec((KEPT_ROWS, TILE_FEATS), lambda tile, step: (step, tile)),
        ],
        out_specs=pl.BlockSpec((sequences, 1, 1, TILE_FEATS), lambda tile, step: (0, tile, 0, 0)),
        out_shape=jax.ShapeDtypeStruct((sequences, features // TILE_FEATS, 1, TILE_FEATS), jnp.float32),
        scratch_shapes=[pltpu.VMEM((DIGITS * sequences, TILE_FEATS), jnp.float32)]
        + [pltpu.VMEM((count, TILE_FEATS), FP8) for count in TILES],
        compiler_params=pltpu.CompilerParams(vmem_limit_bytes=32 << 20),
        cost_estimate=pl.CostEstimate(
            flops=10 * params * features, bytes_accessed=params * features // 4, transcendentals=0
        ),
        name="project",
    )(seeds, direction, scale, kept)


def local(
    hidden_input_rows,
    rank_cotangent,
    token_identifiers,
    adam_first_moment,
    adam_second_moment,
    block_seeds,
):
    groups, device_list = lax.axis_size("groups"), lax.axis_size("dp")
    hidden_width = hidden_input_rows.shape[1]
    rank = rank_cotangent.shape[1]
    rows = adam_first_moment.shape[0] // groups
    half = device_list // 2
    kept_rows = rows * rank // STEP_ROWS * KEPT_ROWS
    early = min(EARLY_ROWS, kept_rows // 3)
    held = (rank_cotangent, token_identifiers)

    given = half_gradient(hidden_input_rows, *held, True, groups, rows)
    pairs = [(source, source ^ 1) for source in range(device_list)]
    other = lax.ppermute(given, "dp", pairs)
    kept = kept_signs(block_seeds, rows, groups, rank, 0, early, EARLY_BLOCK)
    summed = half_gradient(hidden_input_rows, *held, False, groups, rows, other, kept)
    everyone = [
        [group * device_list + 2 * pair + side for group in range(groups) for pair in range(half)]
        for side in range(2)
    ]
    summed = summed.reshape((groups * half,) + summed.shape[2:])
    gradient = lax.all_to_all(
        summed, ("groups", "dp"), split_axis=0, concat_axis=0, axis_index_groups=everyone, tiled=True
    )
    kept = kept_signs(block_seeds, rows, groups, rank, early, kept_rows, LATER_BLOCK, kept)
    direction, scale = scaled_direction(gradient, adam_first_moment, adam_second_moment, rows)
    final_scale = 1.0 / math.sqrt(hidden_width * rank)
    partial = project(block_seeds, direction, scale, kept, rows, groups, rank, final_scale)
    partial = partial.reshape((groups * device_list, 1, TILE_FEATS))
    partial = lax.all_to_all(partial, ("groups", "dp"), split_axis=0, concat_axis=0, tiled=True)
    return jnp.sum(partial, axis=0)


def solution(mesh):
    in_specs = (
        P(("groups", "dp"), None),
        P(("groups", "dp"), None),
        P(("groups", "dp")),
        P("dp", None),
        P("dp", None),
        P(),
    )
    out_specs = P(("groups", "dp"), None)
    return jax.shard_map(local, mesh=mesh, in_specs=in_specs, out_specs=out_specs, check_vma=False)
```

```python
import functools
import math

import jax
import jax.numpy as jnp
from jax import lax
from jax.experimental import pallas as pl
from jax.experimental.pallas import tpu as pltpu
from jax.sharding import PartitionSpec as P

FEAT_BLOCK = 512
beta_one = 0.9
beta_two = 0.999
epsilon = 1e-08
mix_feature = 1640531527
mix_param = 2028178513
mix_round = 73244475
DIGITS = 4
RADIX = 16.0
FP8 = jnp.float8_e4m3fn
STEP_ROWS = 4096
KEPT_ROWS = 1536
TILES = (2304, 256)
EARLY_ROWS, EARLY_BLOCK = 1024, 512
LATER_BLOCK = 512
TILE_FEATS = 2048


def wrap(value):
    value &= 0xFFFFFFFF
    return jnp.int32(value - (1 << 32) if value >= (1 << 31) else value)


def scramble(hashed):
    hashed = hashed ^ lax.shift_right_logical(hashed, jnp.full_like(hashed, 16))
    hashed = hashed * mix_round
    hashed = hashed ^ lax.shift_right_logical(hashed, jnp.full_like(hashed, 16))
    return hashed * mix_round


def strides(rows, rank):
    return (1, rank) if rows % 128 == 0 else (rank, 1)


def minor_size(rows, rank):
    return rows if rows % 128 == 0 else rank


def step_start(rows, rank, groups, step):
    mine = lax.axis_index("dp") * groups + lax.axis_index("groups")
    return mine * (rows * rank) + step * (STEP_ROWS // minor_size(rows, rank) * strides(rows, rank)[0])


def hash_base(seed_ref, feature_tile, start, minor_stride):
    pieces = []
    for piece in range(TILE_FEATS // FEAT_BLOCK):
        block = feature_tile * (TILE_FEATS // FEAT_BLOCK) + piece
        down = lax.broadcasted_iota(jnp.int32, (8, FEAT_BLOCK), 0)
        across = lax.broadcasted_iota(jnp.int32, (8, FEAT_BLOCK), 1)
        scalar = seed_ref[block] + block * wrap(FEAT_BLOCK * mix_feature) + start * wrap(mix_param)
        pieces.append(down * wrap(mix_param * minor_stride) + across * wrap(mix_feature) + scalar)
    return jnp.concatenate(pieces, axis=1)


def write_signs(base, rows, rank, offset, count, out_ref):
    minor, (major_stride, minor_stride) = minor_size(rows, rank), strides(rows, rank)
    for top in range(0, count, 32):
        hashes = []
        for part in range(offset + top, offset + top + 32, 8):
            apart = part // minor * major_stride + part % minor * minor_stride
            hashes.append(scramble(base + wrap(mix_param * apart)))
        hashed = jnp.concatenate(hashes, axis=0)
        out_ref[pl.ds(top, 32), :] = jnp.where(hashed < 0, FP8(-1), FP8(1))


def masked_turned(cotangent, tokens):
    return jnp.where(tokens != 0, cotangent.astype(jnp.float32).T, 0.0).astype(jnp.bfloat16)


def put(result, out_ref, sems, group, pair, piece):
    result[group, pair] = piece
    copy = pltpu.make_async_copy(result.at[group, pair], out_ref.at[group, pair], sems.at[group, pair])
    copy.start()
    return copy


def given_kernel(inputs_ref, cotangent_ref, tokens_ref, out_ref, inputs, cotangent, tokens, result, sems, out_sems):
    groups, pairs, _, rows = out_ref.shape
    width = groups * rows
    side = 1 - (lax.axis_index("dp") & 1)
    small = [
        pltpu.make_async_copy(cotangent_ref, cotangent, sems.at[pairs]),
        pltpu.make_async_copy(tokens_ref, tokens, sems.at[pairs + 1]),
    ]
    large = []
    for pair in range(pairs):
        columns = pl.ds(pl.multiple_of((2 * pair + side) * width, 128), width)
        large.append(pltpu.make_async_copy(inputs_ref.at[:, columns], inputs.at[pair], sems.at[pair]))
    for copy in small + large:
        copy.start()
    for copy in small:
        copy.wait()
    masked = masked_turned(cotangent[...], tokens[...])
    copies = []
    for pair in range(pairs):
        large[pair].wait()
        part = jnp.dot(masked, inputs[pair], preferred_element_type=jnp.float32)
        for group in range(groups):
            copies.append(put(result, out_ref, out_sems, group, pair, part[:, group * rows : (group + 1) * rows]))
    for copy in copies:
        copy.wait()


def summed_kernel(inputs_ref, cotangent_ref, tokens_ref, other_ref, after_ref, out_ref, result, out_sems):
    groups, pairs, _, rows = out_ref.shape
    width = groups * rows
    side = lax.axis_index("dp") & 1
    masked = masked_turned(cotangent_ref[...], tokens_ref[...])
    copies = []
    for pair in range(pairs):
        columns = pl.ds(pl.multiple_of((2 * pair + side) * width, 128), width)
        part = jnp.dot(masked, inputs_ref[:, columns], preferred_element_type=jnp.float32)
        for group in range(groups):
            piece = part[:, group * rows : (group + 1) * rows] + other_ref[group, pair]
            copies.append(put(result, out_ref, out_sems, group, pair, piece))
    for copy in copies:
        copy.wait()


def half_gradient(inputs, cotangent, tokens, away, groups, rows, other=None, after=None):
    count, width = inputs.shape
    rank = cotangent.shape[1]
    pairs = width // (2 * groups * rows)
    if rows % 128:
        side = lax.axis_index("dp") & 1
        side = 1 - side if away else side
        masked = jnp.where((tokens != 0)[:, None], cotangent, jnp.bfloat16(0))
        whole = lax.dot_general(
            inputs, masked, (((0,), (0,)), ((), ())), preferred_element_type=jnp.float32
        )
        whole = whole.reshape(pairs, 2, groups, rows, rank)
        mine = lax.dynamic_index_in_dim(whole, side, 1, keepdims=False).swapaxes(0, 1)
        if away:
            return mine
        other, _ = lax.optimization_barrier((other, after))
        return mine + other
    operands = [inputs, cotangent, tokens[None, :]]
    result = pltpu.VMEM((groups, pairs, rank, rows), jnp.float32)
    out_sems = pltpu.SemaphoreType.DMA((groups, pairs))
    if away:
        in_specs = [pl.BlockSpec(memory_space=pl.ANY)] * 3
        scratch = [
            pltpu.VMEM((pairs, count, groups * rows), jnp.bfloat16),
            pltpu.VMEM((count, rank), jnp.bfloat16),
            pltpu.VMEM((1, count), jnp.int32),
            result,
            pltpu.SemaphoreType.DMA((pairs + 2,)),
            out_sems,
        ]
    else:
        in_specs = [pl.BlockSpec(memory_space=pltpu.VMEM)] * 4 + [pl.BlockSpec(memory_space=pl.ANY)]
        operands += [other, after]
        scratch = [result, out_sems]
    return pl.pallas_call(
        given_kernel if away else summed_kernel,
        in_specs=in_specs,
        out_specs=pl.BlockSpec(memory_space=pl.ANY),
        out_shape=jax.ShapeDtypeStruct((groups, pairs, rank, rows), jnp.float32),
        scratch_shapes=scratch,
        compiler_params=pltpu.CompilerParams(vmem_limit_bytes=None if away else 12 << 20),
        cost_estimate=pl.CostEstimate(
            flops=count * width * rank, bytes_accessed=count * width + 4 * width * rank, transcendentals=0
        ),
        name="half_gradient",
    )(*operands)


def signs_kernel(rows, groups, rank, first, seed_ref, *refs):
    out_ref = refs[-1]
    count = out_ref.shape[0]
    tiles = seed_ref.shape[0] * FEAT_BLOCK // TILE_FEATS
    row = first + pl.program_id(0) // tiles * count
    start = step_start(rows, rank, groups, row // KEPT_ROWS)
    start += row % KEPT_ROWS // minor_size(rows, rank) * strides(rows, rank)[0]
    base = hash_base(seed_ref, pl.program_id(0) % tiles, start, strides(rows, rank)[1])
    write_signs(base, rows, rank, 0, count, out_ref)


def kept_signs(seeds, rows, groups, rank, first, last, block, before=None):
    features = seeds.shape[0] * FEAT_BLOCK
    tiles = features // TILE_FEATS
    size = (last - first) * features
    return pl.pallas_call(
        functools.partial(signs_kernel, rows, groups, rank, first),
        grid=((last - first) // block * tiles,),
        in_specs=[pl.BlockSpec(memory_space=pltpu.SMEM)]
        + [pl.BlockSpec(memory_space=pl.ANY)] * (before is not None),
        out_specs=pl.BlockSpec(
            (block, TILE_FEATS), lambda index: (first // block + index // tiles, index % tiles)
        ),
        out_shape=jax.ShapeDtypeStruct((rows * rank // STEP_ROWS * KEPT_ROWS, features), FP8),
        input_output_aliases={} if before is None else {1: 0},
        compiler_params=pltpu.CompilerParams(vmem_limit_bytes=16 << 20),
        cost_estimate=pl.CostEstimate(flops=size * 10, bytes_accessed=size, transcendentals=0),
        name="kept_signs",
    )(seeds, *([] if before is None else [before]))


def direction_kernel(rows, gradient_ref, first_ref, second_ref, out_ref, scale_ref, held, first, second):
    sequences, major, minor = gradient_ref.shape
    mine = pl.ds(pl.multiple_of(lax.axis_index("groups") * rows, 8), rows)
    turn = major != rows
    first[...] = first_ref[mine, :].T if turn else first_ref[mine, :]
    second[...] = second_ref[mine, :].T if turn else second_ref[mine, :]

    def moments(block, largest):
        at = pl.ds(pl.multiple_of(block * 8, 8), 8)
        gradient = gradient_ref[:, at, :]
        moment_one = beta_one * first[at, :][None] + (1 - beta_one) * gradient
        moment_two = beta_two * second[at, :][None] + (1 - beta_two) * gradient * gradient
        direction = moment_one / (moment_two * lax.rsqrt(moment_two) + epsilon)
        direction = direction.astype(jnp.bfloat16).astype(jnp.float32)
        direction = jnp.swapaxes(direction, 0, 1)
        for row in range(8):
            held[block * 8 + row] = direction[row].astype(jnp.bfloat16)
        return jnp.maximum(largest, jnp.max(jnp.abs(direction), axis=0))

    largest = lax.fori_loop(0, major // 8, moments, jnp.zeros((sequences, minor), jnp.float32), unroll=4)
    largest = jnp.broadcast_to(jnp.max(largest, axis=1, keepdims=True), (sequences, minor))
    scale = jnp.ones_like(largest)
    for power in (64, 32, 16, 8, 4, 2, 1):
        room = largest * (2.0**power) < RADIX
        largest = jnp.where(room, largest * (2.0**power), largest)
        scale = jnp.where(room, scale * (2.0**power), scale)
    for power in (2, 1):
        over = largest >= RADIX
        largest = jnp.where(over, largest * (0.5**power), largest)
        scale = jnp.where(over, scale * (0.5**power), scale)
    scale_ref[...] = scale

    narrow = scale.astype(jnp.bfloat16)
    radix, shift = jnp.bfloat16(RADIX), jnp.bfloat16(192.0)

    def split(row, _):
        rest = held[row] * narrow
        digits = []
        for _ in range(DIGITS):
            digit = (rest + shift) - shift
            digits.append(digit)
            rest = (rest - digit) * radix
        out_ref[:, pl.ds(pl.multiple_of(row * minor, minor), minor)] = jnp.concatenate(digits, axis=0).astype(FP8)
        return 0

    lax.fori_loop(0, major, split, 0, unroll=64)


def scaled_direction(gradient, first, second, rows):
    sequences, major, minor = gradient.shape
    return pl.pallas_call(
        functools.partial(direction_kernel, rows),
        out_shape=(
            jax.ShapeDtypeStruct((DIGITS * sequences, major * minor), FP8),
            jax.ShapeDtypeStruct((sequences, minor), jnp.float32),
        ),
        scratch_shapes=[
            pltpu.VMEM((major, sequences, minor), jnp.bfloat16),
            pltpu.VMEM((major, minor), jnp.float32),
            pltpu.VMEM((major, minor), jnp.float32),
        ],
        compiler_params=pltpu.CompilerParams(vmem_limit_bytes=24 << 20),
        cost_estimate=pl.CostEstimate(
            flops=20 * gradient.size, bytes_accessed=5 * gradient.size, transcendentals=2 * gradient.size
        ),
        name="direction",
    )(gradient, first, second)


def project_kernel(rows, groups, rank, final_scale, seed_ref, direction_ref, scale_ref, kept_ref, out_ref, total, *tiles):
    tile, step = pl.program_id(0), pl.program_id(1)
    sequences = scale_ref.shape[0]
    start = step_start(rows, rank, groups, step)
    last_rows = TILES[-1]

    def multiply(at, signs):
        at = pl.ds(pl.multiple_of(at, 256), signs.shape[0])
        total[...] += jnp.dot(direction_ref[:, at], signs[...], preferred_element_type=jnp.float32)

    @pl.when(step == 0)
    def _():
        total[...] = jnp.zeros_like(total)
        tiles[-1][...] = jnp.zeros_like(tiles[-1])

    here = step * STEP_ROWS
    offset = KEPT_ROWS
    base = hash_base(seed_ref, tile, start, strides(rows, rank)[1])
    for index, count in enumerate(TILES):
        write_signs(base, rows, rank, offset, count, tiles[index])
        if index == 0:
            multiply(jnp.maximum(here - last_rows, 0), tiles[-1])
            multiply(here, kept_ref)
        else:
            multiply(here + offset - TILES[index - 1], tiles[index - 1])
        offset += count

    @pl.when(step == pl.num_programs(1) - 1)
    def _():
        multiply(here + STEP_ROWS - last_rows, tiles[-1])
        inverse = (1.0 / scale_ref[...])[:, :1]
        value = total[(DIGITS - 1) * sequences :, :]
        for digit in reversed(range(DIGITS - 1)):
            value = total[digit * sequences : (digit + 1) * sequences, :] + value * (1.0 / RADIX)
        value = value * inverse * final_scale
        for sequence in range(sequences):
            out_ref[sequence, 0] = value[sequence : sequence + 1, :]


def project(seeds, direction, scale, kept, rows, groups, rank, final_scale):
    features = seeds.shape[0] * FEAT_BLOCK
    sequences = scale.shape[0]
    params = rows * rank
    steps = params // STEP_ROWS
    return pl.pallas_call(
        functools.partial(project_kernel, rows, groups, rank, final_scale),
        grid=(features // TILE_FEATS, steps),
        in_specs=[
            pl.BlockSpec(memory_space=pltpu.SMEM),
            pl.BlockSpec((DIGITS * sequences, params), lambda tile, step: (0, 0)),
            pl.BlockSpec(scale.shape, lambda tile, step: (0, 0)),
            pl.BlockSpec((KEPT_ROWS, TILE_FEATS), lambda tile, step: (step, tile)),
        ],
        out_specs=pl.BlockSpec((sequences, 1, 1, TILE_FEATS), lambda tile, step: (0, tile, 0, 0)),
        out_shape=jax.ShapeDtypeStruct((sequences, features // TILE_FEATS, 1, TILE_FEATS), jnp.float32),
        scratch_shapes=[pltpu.VMEM((DIGITS * sequences, TILE_FEATS), jnp.float32)]
        + [pltpu.VMEM((count, TILE_FEATS), FP8) for count in TILES],
        compiler_params=pltpu.CompilerParams(vmem_limit_bytes=32 << 20),
        cost_estimate=pl.CostEstimate(
            flops=10 * params * features, bytes_accessed=params * features // 4, transcendentals=0
        ),
        name="project",
    )(seeds, direction, scale, kept)


def local(
    hidden_input_rows,
    rank_cotangent,
    token_identifiers,
    adam_first_moment,
    adam_second_moment,
    block_seeds,
):
    groups, device_list = lax.axis_size("groups"), lax.axis_size("dp")
    hidden_width = hidden_input_rows.shape[1]
    rank = rank_cotangent.shape[1]
    rows = adam_first_moment.shape[0] // groups
    half = device_list // 2
    kept_rows = rows * rank // STEP_ROWS * KEPT_ROWS
    early = min(EARLY_ROWS, kept_rows // 3)
    held = (rank_cotangent, token_identifiers)

    given = half_gradient(hidden_input_rows, *held, True, groups, rows)
    pairs = [(source, source ^ 1) for source in range(device_list)]
    other = lax.ppermute(given, "dp", pairs)
    kept = kept_signs(block_seeds, rows, groups, rank, 0, early, EARLY_BLOCK)
    summed = half_gradient(hidden_input_rows, *held, False, groups, rows, other, kept)
    everyone = [
        [group * device_list + 2 * pair + side for group in range(groups) for pair in range(half)]
        for side in range(2)
    ]
    summed = summed.reshape((groups * half,) + summed.shape[2:])
    gradient = lax.all_to_all(
        summed, ("groups", "dp"), split_axis=0, concat_axis=0, axis_index_groups=everyone, tiled=True
    )
    kept = kept_signs(block_seeds, rows, groups, rank, early, kept_rows, LATER_BLOCK, kept)
    direction, scale = scaled_direction(gradient, adam_first_moment, adam_second_moment, rows)
    final_scale = 1.0 / math.sqrt(hidden_width * rank)
    partial = project(block_seeds, direction, scale, kept, rows, groups, rank, final_scale)
    partial = partial.reshape((groups * device_list, 1, TILE_FEATS))
    partial = lax.all_to_all(partial, ("groups", "dp"), split_axis=0, concat_axis=0, tiled=True)
    return jnp.sum(partial, axis=0)


def solution(mesh):
    in_specs = (
        P(("groups", "dp"), None),
        P(("groups", "dp"), None),
        P(("groups", "dp")),
        P("dp", None),
        P("dp", None),
        P(),
    )
    out_specs = P(("groups", "dp"), None)
    return jax.shard_map(local, mesh=mesh, in_specs=in_specs, out_specs=out_specs, check_vma=False)
```
